32 devices in a mesh: group: 2 (over y), dom: 4 (over z), row: 4 (over x, core).
Axes of the slice: x: 2, y: 2, z: 4, core: 2. Of those that a mesh axis runs over, the one named last changes fastest.
Arguments:
- state: bfloat16 [8, 16, 10752], P(('group', 'dom'), 'row'), parts along dimension 0, may hold values from -6 to 6
- prev_pred: bfloat16 [8, 16, 10752], P(('group', 'dom'), 'row'), parts along dimension 0, may hold values from -6 to 6
- ancestors: int32 [8], P('group'), parts along dimension 0, may hold values from 0 to 3, as said below
- timestep: int32 [2], P('group'), parts along dimension 0, may hold values from 50 to 949
- w_in: bfloat16 [168, 256], replicated, may hold values from -0.5 to 0.5
- w_time: bfloat16 [256, 256], replicated, may hold values from -0.375 to 0.375
- w_qkv: bfloat16 [2, 256, 768], replicated, may hold values from -0.375 to 0.375
- w_attn_out: bfloat16 [2, 256, 256], replicated, may hold values from -0.375 to 0.375
- w_up: bfloat16 [2, 256, 1024], replicated, may hold values from -0.375 to 0.375
- w_down: bfloat16 [2, 1024, 256], replicated, may hold values from -0.1875 to 0.1875
- w_out: bfloat16 [256, 84], replicated, may hold values from -0.375 to 0.375
Outputs:
- new_state: bfloat16 [8, 16, 10752], P(('group', 'dom'), 'row'), parts along dimension 0
- new_pred: bfloat16 [8, 16, 10752], P(('group', 'dom'), 'row'), parts along dimension 0
The draws below stay inside these ranges and needn't reach their ends.
There are 2 independent parts, one for each index of `group`. The reference program is written for one: setup_inputs(seed, part) draws one part's arguments, and reference() takes and returns one part's arrays. A program takes and returns all parts, laid end to end along the dimension named above; an argument that names none is the same for every part. Nothing has to cross between parts.
Inputs may be any that keep to these rules, and one draw needn't show every extreme that they name: ancestors[j] is the particle of the same group whose state particle j takes; the list never falls.
All inputs are finite; a program needn't handle non-finite values.
Results may differ from the reference program's by a relative error of at most 0.018.
Values may be sent and summed in bfloat16 or wider, within the bound.
A program may use at most 64 MiB of HBM per device.

```python
import math
import jax
import jax.numpy as jnp
from jax import lax

D = 256
HEADS = 8
FF = 1024
CH = 84
COLS = 128
BLOCKS = 2
STEPS = 1000
STRIDE = 20
PARTICLES = 4
HEIGHT = 16


def draw_ancestors(key, part):
    base_key = jax.random.fold_in(key, 17)
    score_key, offset_key = jax.random.split(base_key)
    levels = jax.random.randint(score_key, (PARTICLES,), 0, 8)
    masses = jnp.left_shift(jnp.ones_like(levels), levels).astype(jnp.int32)
    totals = jnp.cumsum(masses).astype(jnp.int32)
    overall = totals[-1]
    offset = jax.random.randint(offset_key, (), 0, overall)
    points = jnp.arange(PARTICLES, dtype=jnp.int32) * overall + offset
    lineage = jnp.sum((totals[None, :] * PARTICLES <= points[:, None]).astype(jnp.int32), axis=1)
    return lineage.astype(jnp.int32)


def block_scale(key, extent, cuts, low, top_value):
    def one(position, shards_of):
        steps = jax.random.uniform(jax.random.fold_in(jax.random.fold_in(key, 6), position), (shards_of,), jnp.float32, low / len(cuts), top_value / len(cuts))
        return jnp.repeat(jnp.exp(steps), extent[position] // shards_of).reshape((-1,) + (1,) * (len(extent) - position - 1))

    gain = one(*cuts[0])
    for cut in cuts[1:]:
        gain = gain * one(*cut)
    return gain


def gaussian(key, extent, spread, bound, cuts=(), kind=jnp.bfloat16):
    gain = block_scale(key, extent, cuts, -0.22, 0.18) if cuts else 1.0
    values = jax.random.normal(key, extent, jnp.float32) * spread * gain
    return jnp.minimum(jnp.maximum(values, -bound), bound).astype(kind)


def setup_inputs(seed: int = 0, part: int = 0) -> dict:
    key_of = jax.random.split(jax.random.key(seed), 12)
    part_keys = jax.random.split(jax.random.fold_in(key_of[11], part), 12)
    state = gaussian(part_keys[0], (PARTICLES, HEIGHT, COLS * CH), 1.0, 6.0, ((0, 4), (1, 4)))
    prev_pred = gaussian(part_keys[1], (PARTICLES, HEIGHT, COLS * CH), 1.0, 6.0, ((0, 4), (1, 4)))
    ancestors = draw_ancestors(jax.random.fold_in(jax.random.fold_in(key_of[11], part), 71), part)
    timestep = jax.random.randint(part_keys[3], (1,), 50, 950).astype(jnp.int32)
    w_in = gaussian(key_of[4], (2 * CH, D), (2 * CH) ** -0.5, 0.5)
    w_time = gaussian(key_of[5], (D, D), D ** -0.5, 0.375)
    w_qkv = gaussian(key_of[6], (BLOCKS, D, 3 * D), D ** -0.5, 0.375)
    w_attn_out = gaussian(key_of[7], (BLOCKS, D, D), D ** -0.5, 0.375)
    w_up = gaussian(key_of[8], (BLOCKS, D, FF), D ** -0.5, 0.375)
    w_down = gaussian(key_of[9], (BLOCKS, FF, D), FF ** -0.5, 0.1875)
    w_out = gaussian(key_of[10], (D, CH), D ** -0.5, 0.375)
    return {"state": state, "prev_pred": prev_pred, "ancestors": ancestors, "timestep": timestep, "w_in": w_in, "w_time": w_time, "w_qkv": w_qkv, "w_attn_out": w_attn_out, "w_up": w_up, "w_down": w_down, "w_out": w_out}


def rms_round(values_in):
    widened = values_in.astype(jnp.float32)
    scaled = widened * lax.rsqrt(lax.optimization_barrier(jnp.mean(widened * widened, axis=-1, keepdims=True)) + 1e-06)
    return scaled.astype(jnp.bfloat16)

def unit_rows(values_in):
    return values_in * lax.rsqrt(lax.optimization_barrier(jnp.mean(values_in * values_in, axis=-1, keepdims=True)) + 1e-06)

def rotate(values_in, span_len):
    half_size = values_in.shape[-1] // 2
    places = jnp.arange(span_len, dtype=jnp.float32)
    rates = jnp.exp(-math.log(10000.0) * jnp.arange(half_size, dtype=jnp.float32) / half_size)
    angles = places[:, None] * rates[None, :]
    cos_part = jnp.cos(angles)[:, None, None, :]
    sin_part = jnp.sin(angles)[:, None, None, :]
    leading = values_in[..., :half_size]
    trailing = values_in[..., half_size:]
    return jnp.concatenate([leading * cos_part - trailing * sin_part, leading * sin_part + trailing * cos_part], axis=-1)

def attend(normed, weight_qkv, weight_out):
    batch_size, span_len, side_len, model_width = normed.shape
    head_size = model_width // HEADS
    joined = jnp.dot(normed, weight_qkv, preferred_element_type=jnp.float32)
    queries = unit_rows(joined[..., :model_width]).reshape(batch_size, span_len, side_len, HEADS, head_size)
    key_rows = unit_rows(joined[..., model_width:2 * model_width]).reshape(batch_size, span_len, side_len, HEADS, head_size)
    values = joined[..., 2 * model_width:].astype(jnp.bfloat16).reshape(batch_size, span_len, side_len, HEADS, head_size)
    queries = rotate(queries, span_len).astype(jnp.bfloat16)
    key_rows = rotate(key_rows, span_len).astype(jnp.bfloat16)
    scores = jnp.einsum('blmhe,bkmhe->bmhlk', queries.astype(jnp.float32), key_rows.astype(jnp.float32)) / math.sqrt(head_size)
    weights = jnp.exp(scores)
    shares = (weights / lax.optimization_barrier(jnp.sum(weights, axis=-1, keepdims=True))).astype(jnp.bfloat16)
    mixture = jnp.einsum('bmhlk,bkmhe->blmhe', shares.astype(jnp.float32), values.astype(jnp.float32))
    mixture = mixture.astype(jnp.bfloat16).reshape(batch_size, span_len, side_len, model_width)
    return jnp.dot(mixture, weight_out, preferred_element_type=jnp.float32)

def mix_tokens(hidden, weight_qkv, weight_out):
    return (hidden.astype(jnp.float32) + attend(rms_round(hidden), weight_qkv, weight_out)).astype(jnp.bfloat16)

def feed_forward(hidden, weight_up, weight_down):
    lifted = jnp.dot(rms_round(hidden), weight_up, preferred_element_type=jnp.float32)
    gated = jax.nn.gelu(lifted, approximate=True).astype(jnp.bfloat16)
    return (hidden.astype(jnp.float32) + jnp.dot(gated, weight_down, preferred_element_type=jnp.float32)).astype(jnp.bfloat16)

def level(moment):
    cosine = jnp.cos((moment / STEPS + 0.008) / 1.008 * math.pi / 2.0)
    return cosine * cosine

def time_vector(timestep, w_time):
    moment = timestep[0].astype(jnp.float32)
    half_size = w_time.shape[0] // 2
    rates = jnp.exp(-math.log(10000.0) * jnp.arange(half_size, dtype=jnp.float32) / half_size)
    embedded = jnp.concatenate([jnp.sin(moment * rates), jnp.cos(moment * rates)])
    return jnp.dot(embedded, w_time.astype(jnp.float32), precision=lax.Precision.HIGHEST)

def reference(state, prev_pred, ancestors, timestep, w_in, w_time, w_qkv, w_attn_out, w_up, w_down, w_out):
    offset_vec = time_vector(timestep, w_time)
    moment = timestep[0].astype(jnp.float32)
    level_now = level(moment)
    level_next = level(moment - STRIDE)
    chosen_state = jnp.take(state, ancestors, axis=0)
    chosen_prev = jnp.take(prev_pred, ancestors, axis=0)

    def denoise(pieces):
        state_rows, prev_rows = pieces
        height_len = state_rows.shape[0]
        joined = jnp.concatenate([state_rows.reshape(height_len, COLS, CH), prev_rows.reshape(height_len, COLS, CH)], axis=-1)
        hidden = (jnp.dot(joined, w_in, preferred_element_type=jnp.float32) + offset_vec).astype(jnp.bfloat16)
        hidden = hidden[:, :, None, :]
        hidden = mix_tokens(hidden, w_qkv[0], w_attn_out[0])
        hidden = feed_forward(hidden, w_up[0], w_down[0])
        hidden = hidden.reshape(1, height_len, COLS, hidden.shape[-1])
        hidden = mix_tokens(hidden, w_qkv[1], w_attn_out[1])
        hidden = feed_forward(hidden, w_up[1], w_down[1])
        predicted = jnp.dot(rms_round(hidden), w_out, preferred_element_type=jnp.float32).astype(jnp.bfloat16)
        predicted = predicted.reshape(height_len, COLS * CH)
        widened = state_rows.astype(jnp.float32)
        pred_wide = predicted.astype(jnp.float32)
        noise_est = (widened - jnp.sqrt(level_now) * pred_wide) / jnp.sqrt(1.0 - level_now)
        updated = (jnp.sqrt(level_next) * pred_wide + jnp.sqrt(1.0 - level_next) * noise_est).astype(jnp.bfloat16)
        return (updated, predicted)
    new_state, new_pred = lax.map(denoise, (chosen_state, chosen_prev))
    return (new_state, new_pred)
```

```python
import functools
import math

import jax
import jax.numpy as jnp
import numpy as np
from jax import lax
from jax.experimental import pallas as pl
from jax.experimental.pallas import tpu as pltpu
from jax.sharding import PartitionSpec as P

HEADS = 8
STEPS = 1000
STRIDE = 20
LANES = 128
MESH = pl.DeviceIdType.MESH
F32 = jnp.float32
BF16 = jnp.bfloat16


def rms(v):
    return v * lax.rsqrt(jnp.mean(v * v, axis=-1, keepdims=True) + 1e-06)


def mm(a, b):
    return jnp.dot(a, b, preferred_element_type=F32)


def mm_nt(a, b):
    return lax.dot_general(a, b, (((1,), (1,)), ((), ())), preferred_element_type=F32)


def rope_tables(length, head):
    half = head // 2
    rates = np.exp(-math.log(10000.0) * np.arange(half) / half)
    angles = np.arange(length)[:, None] * rates[None, :]
    reps = LANES // head
    cos = np.tile(np.concatenate([np.cos(angles), np.cos(angles)], axis=1), (1, reps))
    sin = np.tile(np.concatenate([-np.sin(angles), np.sin(angles)], axis=1), (1, reps))
    return cos.astype(np.float32), sin.astype(np.float32)


def rotated(v, cos, sin, head):
    inv = lax.rsqrt(jnp.mean(v * v, axis=-1, keepdims=True) + 1e-06)
    lane = lax.broadcasted_iota(jnp.int32, (1, LANES), 1)
    low = (lane % head) < head // 2
    parts = []
    for part in range(v.shape[1] // LANES):
        x = v[:, part * LANES : (part + 1) * LANES]
        partner = jnp.where(
            low,
            pltpu.roll(x, LANES - head // 2, 1),
            pltpu.roll(x, head // 2, 1),
        )
        parts.append((x * cos + partner * sin) * inv)
    return parts


def attention(q, k, v, mask, head):
    n = q[0].shape[0]
    lane = lax.broadcasted_iota(jnp.int32, (1, LANES), 1)
    per = LANES // head
    scale = math.log2(math.e) / math.sqrt(head)
    outs = []
    for part in range(len(q)):
        keys, vals = [], []
        for h in range(per):
            pick = jnp.where(lane // head == h, 1.0, 0.0).astype(BF16)
            keys.append(k[part] * pick)
            vals.append(
                jnp.concatenate([v[part] * pick, jnp.broadcast_to(pick, (n, LANES))], axis=1)
            )
        scores = mm_nt(q[part], jnp.concatenate(keys, axis=0))
        weights = jnp.exp2(scores * scale)
        if mask is not None:
            weights = weights * mask
        both = mm(weights.astype(BF16), jnp.concatenate(vals, axis=0))
        outs.append(both[:, :LANES] / both[:, LANES:])
    return jnp.concatenate(outs, axis=1).astype(BF16)


def mlp(h, w_up, w_down):
    lifted = mm(rms(h).astype(BF16), w_up)
    gated = jax.nn.gelu(lifted, approximate=True).astype(BF16)
    return (h + mm(gated, w_down)).astype(BF16)


def kernel(
    cfg,
    anc_ref, coef_ref, state_ref, prev_ref, emb_ref, tab_ref, w_in_ref, w_time_ref,
    w_qkv_hbm, w_attn_hbm, w_up_hbm, w_down_hbm, w_out_ref,
    new_state_ref, new_pred_ref,
    w_qkv, w_attn, w_up, w_down,
    xs, xp, h1, hcol, psend, ptok, states, preds,
    w_sem, own_sem, st_send, st_recv, h_send, h_recv, p_send, p_recv, g_send, g_recv,
):
    ndom, nrow, rows, cols, ch, d, head, height = cfg
    dom, row = lax.axis_index("dom"), lax.axis_index("row")
    mine = cols // nrow
    width = cols * ch
    group = LANES // math.gcd(ch, LANES)
    glanes = group * ch

    loads = []
    pairs = ((w_qkv_hbm, w_qkv), (w_attn_hbm, w_attn), (w_up_hbm, w_up), (w_down_hbm, w_down))
    for b in range(2):
        for i, (src, dst) in enumerate(pairs):
            copy = pltpu.make_async_copy(src.at[b], dst.at[b], w_sem.at[b, i])
            copy.start()
            loads.append(copy)

    barrier = pltpu.get_barrier_semaphore()
    for k in range(1, ndom):
        pl.semaphore_signal(
            barrier, inc=1, device_id={"dom": lax.rem(dom + k, ndom)}, device_id_type=MESH
        )
    for k in range(1, nrow):
        pl.semaphore_signal(
            barrier, inc=1, device_id={"row": lax.rem(row + k, nrow)}, device_id_type=MESH
        )
    own = pltpu.make_async_copy(state_ref.at[0], states.at[dom], own_sem)
    own.start()

    lane = lax.broadcasted_iota(jnp.int32, (rows, LANES), 1)

    def split(c, carry):
        base = pl.multiple_of(c * glanes, LANES)
        for ref, out in ((state_ref, xs), (prev_ref, xp)):
            tiles = [
                ref[0, :, pl.ds(pl.multiple_of(base + j * LANES, LANES), LANES)].astype(F32)
                for j in range(glanes // LANES)
            ]
            for t in range(group):
                j, off = divmod(t * ch, LANES)
                v = pltpu.roll(tiles[j], LANES - off, 1) if off else tiles[j]
                if off + ch > LANES:
                    v = jnp.where(lane < LANES - off, v, pltpu.roll(tiles[j + 1], LANES - off, 1))
                out[pl.ds(c * group + t, rows, stride=cols), :] = v
        return carry

    lax.fori_loop(0, cols // group, split, 0)

    pl.semaphore_wait(barrier, ndom - 1 + nrow - 1)
    sends = []
    for k in range(1, ndom):
        copy = pltpu.make_async_remote_copy(
            src_ref=state_ref.at[0],
            dst_ref=states.at[dom],
            send_sem=st_send.at[k],
            recv_sem=st_recv.at[k],
            device_id={"dom": lax.rem(dom + k, ndom)},
            device_id_type=MESH,
        )
        copy.start()
        sends.append(copy)

    temb = jnp.dot(
        emb_ref[...], w_time_ref[...].astype(F32),
        precision=lax.Precision.HIGHEST, preferred_element_type=F32,
    )[0:1]
    w_in = w_in_ref[...].astype(F32)
    w_in_s, w_in_p = w_in[:ch].astype(BF16), w_in[ch:].astype(BF16)

    for copy in loads[:4]:
        copy.wait()
    cos_r, sin_r = tab_ref[0:cols], tab_ref[cols : 2 * cols]
    step_rows = 2 if rows % 2 == 0 else 1
    n0 = step_rows * cols

    def first(i, carry):
        sl = pl.ds(pl.multiple_of(i * n0, n0), n0)
        h = mm(xs[sl, :ch].astype(BF16), w_in_s) + mm(xp[sl, :ch].astype(BF16), w_in_p) + temb
        h = h.astype(BF16).astype(F32)
        qkv = mm(rms(h).astype(BF16), w_qkv[0])
        cos = jnp.concatenate([cos_r] * step_rows, axis=0)
        sin = jnp.concatenate([sin_r] * step_rows, axis=0)
        q = [x.astype(BF16) for x in rotated(qkv[:, :d], cos, sin, head)]
        k = [x.astype(BF16) for x in rotated(qkv[:, d : 2 * d], cos, sin, head)]
        v = qkv[:, 2 * d :].astype(BF16)
        v = [v[:, p * LANES : (p + 1) * LANES] for p in range(d // LANES)]
        mixed = []
        for r in range(step_rows):
            a, b = r * cols, (r + 1) * cols
            mixed.append(
                attention([x[a:b] for x in q], [x[a:b] for x in k], [x[a:b] for x in v], None, head)
            )
        o = jnp.concatenate(mixed, axis=0)
        h = (h + mm(o, w_attn[0])).astype(BF16).astype(F32)
        h = mlp(h, w_up[0], w_down[0])
        h1[pl.ds(i * step_rows, step_rows)] = h.reshape(step_rows, cols, d)
        return carry

    lax.fori_loop(0, rows // step_rows, first, 0)

    hs = []
    for k in range(1, nrow):
        peer = lax.rem(row + k, nrow)
        copy = pltpu.make_async_remote_copy(
            src_ref=h1.at[:, pl.ds(pl.multiple_of(peer * mine, mine), mine), :],
            dst_ref=hcol.at[pl.ds(row * rows, rows)],
            send_sem=h_send.at[k],
            recv_sem=h_recv.at[k],
            device_id={"row": peer},
            device_id_type=MESH,
        )
        copy.start()
        hs.append(copy)
    hcol[pl.ds(row * rows, rows)] = h1[:, pl.ds(pl.multiple_of(row * mine, mine), mine), :]
    for copy in loads[4:]:
        copy.wait()
    for copy in hs:
        copy.wait_recv()

    cos_c = tab_ref[2 * cols : 2 * cols + 8 * height].reshape(height, 8, LANES)
    sin_c = tab_ref[2 * cols + 8 * height : 2 * cols + 16 * height].reshape(height, 8, LANES)
    wide = 16
    n1 = height * wide
    sub = height * 8
    cos_c = jnp.concatenate([cos_c, cos_c], axis=1).reshape(n1, LANES)
    sin_c = jnp.concatenate([sin_c, sin_c], axis=1).reshape(n1, LANES)
    per = LANES // head
    qi = lax.broadcasted_iota(jnp.int32, (sub, per * sub), 0)
    ki = lax.broadcasted_iota(jnp.int32, (sub, per * sub), 1)
    mask = jnp.where(qi % 8 == ki % 8, 1.0, 0.0).astype(F32)

    def second(i, carry):
        sl = pl.ds(pl.multiple_of(i * wide, wide), wide)
        h = hcol[:, sl, :].reshape(n1, d).astype(F32)
        qkv = mm(rms(h).astype(BF16), w_qkv[1])
        q = rotated(qkv[:, :d], cos_c, sin_c, head)
        k = rotated(qkv[:, d : 2 * d], cos_c, sin_c, head)
        v = [qkv[:, 2 * d + p * LANES : 2 * d + (p + 1) * LANES] for p in range(d // LANES)]
        mixed = []
        for s in range(wide // 8):

            def cut(xs_):
                return [
                    x.reshape(height, wide, LANES)[:, 8 * s : 8 * s + 8, :]
                    .reshape(sub, LANES)
                    .astype(BF16)
                    for x in xs_
                ]

            o = attention(cut(q), cut(k), cut(v), mask, head)
            mixed.append(o.astype(F32).reshape(height, 8, d))
        o = jnp.concatenate(mixed, axis=1).reshape(n1, d).astype(BF16)
        h = (h + mm(o, w_attn[1])).astype(BF16).astype(F32)
        h = mlp(h, w_up[1], w_down[1]).astype(F32)
        pred = mm(rms(h).astype(BF16), w_out_ref[...])
        psend[:, sl, 0:ch] = pred.astype(BF16).reshape(height, wide, ch)
        return carry

    lax.fori_loop(0, mine // wide, second, 0)

    ps = []
    for k in range(1, nrow):
        peer = lax.rem(row + k, nrow)
        copy = pltpu.make_async_remote_copy(
            src_ref=psend.at[pl.ds(peer * rows, rows)],
            dst_ref=ptok.at[:, pl.ds(pl.multiple_of(row * mine, mine), mine), :],
            send_sem=p_send.at[k],
            recv_sem=p_recv.at[k],
            device_id={"row": peer},
            device_id_type=MESH,
        )
        copy.start()
        ps.append(copy)
    ptok[:, pl.ds(pl.multiple_of(row * mine, mine), mine), :] = psend[pl.ds(row * rows, rows)]
    for copy in ps:
        copy.wait_recv()
    for r in range(rows):
        xs[r * cols : (r + 1) * cols, :] = ptok[r].astype(F32)

    def join(c, carry):
        base = c * glanes
        toks = [xs[pl.ds(c * group + t, rows, stride=cols), :] for t in range(group)]
        for j in range(glanes // LANES):
            first_t, last_t = (j * LANES) // ch, (j * LANES + LANES - 1) // ch
            acc = None
            for t in range(first_t, last_t + 1):
                s = t * ch - j * LANES
                v = pltpu.roll(toks[t], s % LANES, 1) if s % LANES else toks[t]
                acc = v if acc is None else jnp.where(lane >= s, v, acc)
            preds[dom, :, pl.ds(pl.multiple_of(base + j * LANES, LANES), LANES)] = acc.astype(BF16)
        return carry

    lax.fori_loop(0, cols // group, join, 0)

    gs = []
    for k in range(1, ndom):
        copy = pltpu.make_async_remote_copy(
            src_ref=preds.at[dom],
            dst_ref=preds.at[dom],
            send_sem=g_send.at[k],
            recv_sem=g_recv.at[k],
            device_id={"dom": lax.rem(dom + k, ndom)},
            device_id_type=MESH,
        )
        copy.start()
        gs.append(copy)
    own.wait()
    for copy in sends:
        copy.wait()
    for copy in gs:
        copy.wait()
    for copy in hs + ps:
        copy.wait_send()
    a = anc_ref[dom]
    c1, c2, c3 = coef_ref[0], coef_ref[1], coef_ref[2]
    for c in range(cols // group):
        sl = pl.ds(c * glanes, glanes)
        p = preds[a, :, sl]
        pw = p.astype(F32)
        st = states[a, :, sl].astype(F32)
        new_pred_ref[0, :, sl] = p
        new_state_ref[0, :, sl] = (c2 * pw + c3 * (st - c1 * pw)).astype(BF16)


def level(moment):
    cosine = jnp.cos((moment / STEPS + 0.008) / 1.008 * math.pi / 2.0)
    return cosine * cosine


def per_device(
    sizes, state, prev_pred, ancestors, timestep, w_in, w_time, w_qkv, w_attn_out, w_up, w_down, w_out
):
    ndom, nrow = sizes
    _, rows, width = state.shape
    d, ch = w_out.shape
    cols, height, head = width // ch, rows * nrow, d // HEADS
    ff = w_up.shape[2]
    moment = timestep[0].astype(F32)
    half = w_time.shape[0] // 2
    rates = jnp.exp(-math.log(10000.0) * jnp.arange(half, dtype=F32) / half)
    emb = jnp.concatenate([jnp.sin(moment * rates), jnp.cos(moment * rates)])
    emb = jnp.broadcast_to(emb[None], (8, 2 * half))
    now, nxt = level(moment), level(moment - STRIDE)
    coef = jnp.stack([jnp.sqrt(now), jnp.sqrt(nxt), jnp.sqrt(1.0 - nxt) / jnp.sqrt(1.0 - now)])
    cos_r, sin_r = rope_tables(cols, head)
    cos_c, sin_c = rope_tables(height, head)
    tables = jnp.asarray(
        np.concatenate([cos_r, sin_r, np.repeat(cos_c, 8, axis=0), np.repeat(sin_c, 8, axis=0)])
    )
    cfg = (ndom, nrow, rows, cols, ch, d, head, height)
    mine = cols // nrow
    smem = pl.BlockSpec(memory_space=pltpu.SMEM)
    vmem = pl.BlockSpec(memory_space=pltpu.VMEM)
    hbm = pl.BlockSpec(memory_space=pl.ANY)
    flat = jax.ShapeDtypeStruct((1, rows, width), BF16)
    dma = pltpu.SemaphoreType.DMA
    return pl.pallas_call(
        functools.partial(kernel, cfg),
        out_shape=(flat, flat),
        in_specs=[smem, smem, vmem, vmem, vmem, vmem, vmem, vmem, hbm, hbm, hbm, hbm, vmem],
        out_specs=(vmem, vmem),
        scratch_shapes=[
            pltpu.VMEM((2, d, 3 * d), BF16),
            pltpu.VMEM((2, d, d), BF16),
            pltpu.VMEM((2, d, ff), BF16),
            pltpu.VMEM((2, ff, d), BF16),
            pltpu.VMEM((rows * cols, LANES), F32),
            pltpu.VMEM((rows * cols, LANES), F32),
            pltpu.VMEM((rows, cols, d), BF16),
            pltpu.VMEM((height, mine, d), BF16),
            pltpu.VMEM((height, mine, LANES), BF16),
            pltpu.VMEM((rows, cols, LANES), BF16),
            pltpu.VMEM((ndom, rows, width), BF16),
            pltpu.VMEM((ndom, rows, width), BF16),
            dma((2, 4)),
            dma,
            dma((ndom,)),
            dma((ndom,)),
            dma((nrow,)),
            dma((nrow,)),
            dma((nrow,)),
            dma((nrow,)),
            dma((ndom,)),
            dma((ndom,)),
        ],
        compiler_params=pltpu.CompilerParams(
            collective_id=0, has_side_effects=True, vmem_limit_bytes=56 * 1024 * 1024
        ),
    )(
        ancestors, coef, state, prev_pred, emb, tables, w_in, w_time,
        w_qkv, w_attn_out, w_up, w_down, w_out,
    )


def solution(mesh):
    part = P(("group", "dom"), "row", None)
    in_specs = (part, part, P("group"), P("group")) + (P(),) * 7
    return jax.shard_map(
        functools.partial(per_device, (mesh.shape["dom"], mesh.shape["row"])),
        mesh=mesh, in_specs=in_specs, out_specs=(part, part), check_vma=False,
    )
```

```python
import functools
import math

import jax
import jax.numpy as jnp
import numpy as np
from jax import lax
from jax.experimental import pallas as pl
from jax.experimental.pallas import tpu as pltpu
from jax.sharding import PartitionSpec as P

HEADS = 8
STEPS = 1000
STRIDE = 20
LANES = 128
MESH = pl.DeviceIdType.MESH
F32 = jnp.float32
BF16 = jnp.bfloat16


def rms(v):
    return v * lax.rsqrt(jnp.mean(v * v, axis=-1, keepdims=True) + 1e-06)


def mm(a, b):
    return jnp.dot(a, b, preferred_element_type=F32)


def mm_nt(a, b):
    return lax.dot_general(a, b, (((1,), (1,)), ((), ())), preferred_element_type=F32)


def rope_tables(length, head):
    half = head // 2
    rates = np.exp(-math.log(10000.0) * np.arange(half) / half)
    angles = np.arange(length)[:, None] * rates[None, :]
    reps = LANES // head
    cos = np.tile(np.concatenate([np.cos(angles), np.cos(angles)], axis=1), (1, reps))
    sin = np.tile(np.concatenate([-np.sin(angles), np.sin(angles)], axis=1), (1, reps))
    return cos.astype(np.float32), sin.astype(np.float32)


def rotated(v, cos, sin, head):
    inv = lax.rsqrt(jnp.mean(v * v, axis=-1, keepdims=True) + 1e-06)
    lane = lax.broadcasted_iota(jnp.int32, (1, LANES), 1)
    low = (lane % head) < head // 2
    parts = []
    for part in range(v.shape[1] // LANES):
        x = v[:, part * LANES : (part + 1) * LANES]
        partner = jnp.where(
            low,
            pltpu.roll(x, LANES - head // 2, 1),
            pltpu.roll(x, head // 2, 1),
        )
        parts.append((x * cos + partner * sin) * inv)
    return parts


def attention(q, k, v, mask, head):
    n = q[0].shape[0]
    lane = lax.broadcasted_iota(jnp.int32, (1, LANES), 1)
    per = LANES // head
    scale = math.log2(math.e) / math.sqrt(head)
    outs = []
    for part in range(len(q)):
        keys, vals = [], []
        for h in range(per):
            pick = jnp.where(lane // head == h, 1.0, 0.0).astype(BF16)
            keys.append(k[part] * pick)
            vals.append(
                jnp.concatenate([v[part] * pick, jnp.broadcast_to(pick, (n, LANES))], axis=1)
            )
        scores = mm_nt(q[part], jnp.concatenate(keys, axis=0))
        weights = jnp.exp2(scores * scale)
        if mask is not None:
            weights = weights * mask
        both = mm(weights.astype(BF16), jnp.concatenate(vals, axis=0))
        outs.append(both[:, :LANES] / both[:, LANES:])
    return jnp.concatenate(outs, axis=1).astype(BF16)


def mlp(h, w_up, w_down):
    lifted = mm(rms(h).astype(BF16), w_up)
    gated = jax.nn.gelu(lifted, approximate=True).astype(BF16)
    return (h + mm(gated, w_down)).astype(BF16)


def kernel(
    cfg,
    anc_ref, time_ref, state_ref, prev_ref, tab_ref, w_in_ref, w_time_ref,
    w_qkv_hbm, w_attn_hbm, w_up_hbm, w_down_hbm, w_out_ref,
    state_out, pred_out,
    w_qkv, w_attn, w_up, w_down,
    xs, xp, h1, hcol, ptok, gat, selw, sel, fin, states,
    w_sem, own_sem, st_send, st_recv, h_send, h_recv, g_send, g_recv, p_send, p_recv,
):
    ndom, nrow, rows, cols, ch, d, head, height, wide, flat = cfg
    dom, row = lax.axis_index("dom"), lax.axis_index("row")
    mine = cols // nrow
    group = LANES // math.gcd(ch, LANES)
    glanes = group * ch
    halves = mine // wide

    loads = []
    pairs = ((w_qkv_hbm, w_qkv), (w_attn_hbm, w_attn), (w_up_hbm, w_up), (w_down_hbm, w_down))
    for b in range(2):
        for i, (src, dst) in enumerate(pairs):
            copy = pltpu.make_async_copy(src.at[b], dst.at[b], w_sem.at[b, i])
            copy.start()
            loads.append(copy)

    barrier = pltpu.get_barrier_semaphore()
    for k in range(1, ndom):
        pl.semaphore_signal(
            barrier, inc=1, device_id={"dom": lax.rem(dom + k, ndom)}, device_id_type=MESH
        )
    for k in range(1, nrow):
        pl.semaphore_signal(
            barrier, inc=1, device_id={"row": lax.rem(row + k, nrow)}, device_id_type=MESH
        )
    own = pltpu.make_async_copy(state_ref.at[0], states.at[dom], own_sem)
    own.start()

    lane = lax.broadcasted_iota(jnp.int32, (rows, LANES), 1)

    def split(c, carry):
        base = pl.multiple_of(c * glanes, LANES)
        for ref, out in ((state_ref, xs), (prev_ref, xp)):
            tiles = [
                ref[0, :, pl.ds(pl.multiple_of(base + j * LANES, LANES), LANES)].astype(F32)
                for j in range(glanes // LANES)
            ]
            for t in range(group):
                j, off = divmod(t * ch, LANES)
                v = pltpu.roll(tiles[j], LANES - off, 1) if off else tiles[j]
                if off + ch > LANES:
                    v = jnp.where(lane < LANES - off, v, pltpu.roll(tiles[j + 1], LANES - off, 1))
                out[pl.ds(c * group + t, rows, stride=cols), :] = v
        return carry

    lax.fori_loop(0, cols // group, split, 0)

    moment = time_ref[0].astype(F32)
    half = d // 2
    angles = tab_ref[2 * cols + 16 * height :, :] * moment
    emb = jnp.concatenate([jnp.sin(angles), jnp.cos(angles)], axis=1)
    temb = jnp.dot(
        emb, w_time_ref[...].astype(F32),
        precision=lax.Precision.HIGHEST, preferred_element_type=F32,
    )[0:1]
    w_in = w_in_ref[...].astype(F32)
    w_in_s, w_in_p = w_in[:ch].astype(BF16), w_in[ch:].astype(BF16)

    pl.semaphore_wait(barrier, ndom - 1 + nrow - 1)
    sends = []
    for k in range(1, ndom):
        copy = pltpu.make_async_remote_copy(
            src_ref=state_ref.at[0],
            dst_ref=states.at[dom],
            send_sem=st_send.at[k],
            recv_sem=st_recv.at[k],
            device_id={"dom": lax.rem(dom + k, ndom)},
            device_id_type=MESH,
        )
        copy.start()
        sends.append(copy)

    for copy in loads[:4]:
        copy.wait()
    cos_r, sin_r = tab_ref[0:cols], tab_ref[cols : 2 * cols]
    step_rows = 2 if rows % 2 == 0 else 1
    n0 = step_rows * cols

    def h_copy(i, k):
        peer = lax.rem(row + k, nrow)
        return pltpu.make_async_remote_copy(
            src_ref=h1.at[pl.ds(i * step_rows, step_rows), pl.ds(pl.multiple_of(peer * mine, mine), mine), :],
            dst_ref=hcol.at[pl.ds(row * rows + i * step_rows, step_rows)],
            send_sem=h_send.at[i, k],
            recv_sem=h_recv.at[i, k],
            device_id={"row": peer},
            device_id_type=MESH,
        )

    def first(i, carry):
        sl = pl.ds(pl.multiple_of(i * n0, n0), n0)
        h = mm(xs[sl, :ch].astype(BF16), w_in_s) + mm(xp[sl, :ch].astype(BF16), w_in_p) + temb
        h = h.astype(BF16).astype(F32)
        qkv = mm(rms(h).astype(BF16), w_qkv[0])
        cos = jnp.concatenate([cos_r] * step_rows, axis=0)
        sin = jnp.concatenate([sin_r] * step_rows, axis=0)
        q = [x.astype(BF16) for x in rotated(qkv[:, :d], cos, sin, head)]
        k = [x.astype(BF16) for x in rotated(qkv[:, d : 2 * d], cos, sin, head)]
        v = qkv[:, 2 * d :].astype(BF16)
        v = [v[:, p * LANES : (p + 1) * LANES] for p in range(d // LANES)]
        mixed = []
        for r in range(step_rows):
            a, b = r * cols, (r + 1) * cols
            mixed.append(
                attention([x[a:b] for x in q], [x[a:b] for x in k], [x[a:b] for x in v], None, head)
            )
        o = jnp.concatenate(mixed, axis=0)
        h = (h + mm(o, w_attn[0])).astype(BF16).astype(F32)
        h = mlp(h, w_up[0], w_down[0])
        h1[pl.ds(i * step_rows, step_rows)] = h.reshape(step_rows, cols, d)
        for k in range(1, nrow):
            h_copy(i, k).start()
        return carry

    lax.fori_loop(0, rows // step_rows, first, 0)

    hcol[pl.ds(row * rows, rows)] = h1[:, pl.ds(pl.multiple_of(row * mine, mine), mine), :]
    for copy in loads[4:]:
        copy.wait()

    cos_c = tab_ref[2 * cols : 2 * cols + 8 * height].reshape(height, 8, LANES)
    sin_c = tab_ref[2 * cols + 8 * height : 2 * cols + 16 * height].reshape(height, 8, LANES)
    n1 = height * wide
    sub = height * 8
    cos_c = jnp.concatenate([cos_c] * (wide // 8), axis=1).reshape(n1, LANES)
    sin_c = jnp.concatenate([sin_c] * (wide // 8), axis=1).reshape(n1, LANES)
    per = LANES // head
    qi = lax.broadcasted_iota(jnp.int32, (sub, per * sub), 0)
    ki = lax.broadcasted_iota(jnp.int32, (sub, per * sub), 1)
    mask = jnp.where(qi % 8 == ki % 8, 1.0, 0.0).astype(F32)
    hlane = lax.broadcasted_iota(jnp.int32, (height, LANES), 1)

    for i in range(rows // step_rows):
        for k in range(1, nrow):
            h_copy(i, k).wait_recv()

    def g_copy(i, k):
        return pltpu.make_async_remote_copy(
            src_ref=gat[i].at[dom],
            dst_ref=gat[i].at[dom],
            send_sem=g_send.at[i, k],
            recv_sem=g_recv.at[i, k],
            device_id={"dom": lax.rem(dom + k, ndom)},
            device_id_type=MESH,
        )

    def second(i):
        sl = pl.ds(i * wide, wide)
        h = hcol[:, sl, :].reshape(n1, d).astype(F32)
        qkv = mm(rms(h).astype(BF16), w_qkv[1])
        q = rotated(qkv[:, :d], cos_c, sin_c, head)
        k = rotated(qkv[:, d : 2 * d], cos_c, sin_c, head)
        v = [qkv[:, 2 * d + p * LANES : 2 * d + (p + 1) * LANES] for p in range(d // LANES)]
        mixed = []
        for s in range(wide // 8):

            def cut(xs_):
                return [
                    x.reshape(height, wide, LANES)[:, 8 * s : 8 * s + 8, :]
                    .reshape(sub, LANES)
                    .astype(BF16)
                    for x in xs_
                ]

            o = attention(cut(q), cut(k), cut(v), mask, head)
            mixed.append(o.astype(F32).reshape(height, 8, d))
        o = jnp.concatenate(mixed, axis=1).reshape(n1, d).astype(BF16)
        h = (h + mm(o, w_attn[1])).astype(BF16).astype(F32)
        h = mlp(h, w_up[1], w_down[1]).astype(F32)
        ptok[:, 0:ch] = mm_nt(rms(h).astype(BF16), w_out_ref[...])
        toks = [ptok[pl.ds(t, height, stride=wide), :] for t in range(wide)]
        for j in range(flat // LANES):
            first_t = (j * LANES) // ch
            last_t = min((j * LANES + LANES - 1) // ch, wide - 1)
            acc = None
            for t in range(first_t, last_t + 1):
                s = t * ch - j * LANES
                x = pltpu.roll(toks[t], s % LANES, 1) if s % LANES else toks[t]
                acc = x if acc is None else jnp.where(hlane >= s, x, acc)
            gat[i][dom, :, j * LANES : (j + 1) * LANES] = acc.astype(BF16)
        for k in range(1, ndom):
            g_copy(i, k).start()

    for i in range(halves):
        second(i)

    own.wait()
    for copy in sends:
        copy.wait()
    a = anc_ref[dom]
    state_out[0] = states[a]

    def p_copy(i, k):
        peer = lax.rem(row + k, nrow)
        return pltpu.make_async_remote_copy(
            src_ref=sel.at[i, peer],
            dst_ref=fin.at[row, i],
            send_sem=p_send.at[i, k],
            recv_sem=p_recv.at[i, k],
            device_id={"row": peer},
            device_id_type=MESH,
        )

    for i in range(halves):
        for k in range(1, ndom):
            g_copy(i, k).wait_recv()
        selw[...] = gat[i][a].astype(F32)
        for r in range(nrow):
            sel[i, r] = selw[r * rows : (r + 1) * rows, :].astype(BF16)
        for k in range(1, nrow):
            p_copy(i, k).start()
        fin[row, i] = sel[i, row]
    for i in range(halves):
        for k in range(1, nrow):
            p_copy(i, k).wait_recv()

    size = wide * ch
    count = flat // LANES

    def piece(q, offset):
        r, i = divmod(q, halves)
        tile, rem = divmod(offset, LANES)

        def load(j):
            x = fin[r, i, :, j * LANES : (j + 1) * LANES].astype(F32)
            return pltpu.roll(x, LANES - rem, 1) if rem else x

        low = load(tile) if tile >= 0 else None
        if not rem or tile + 1 >= count:
            return low
        high = load(tile + 1)
        return high if low is None else jnp.where(lane < LANES - rem, low, high)

    for j in range(cols * ch // LANES):
        start = j * LANES
        acc = None
        for q in range(start // size, (start + LANES - 1) // size + 1):
            x = piece(q, start - q * size)
            acc = x if acc is None else jnp.where(lane >= q * size - start, x, acc)
        pred_out[0, :, start : start + LANES] = acc.astype(BF16)

    for i in range(rows // step_rows):
        for k in range(1, nrow):
            h_copy(i, k).wait_send()
    for i in range(halves):
        for k in range(1, ndom):
            g_copy(i, k).wait_send()
        for k in range(1, nrow):
            p_copy(i, k).wait_send()


def level(moment):
    cosine = jnp.cos((moment / STEPS + 0.008) / 1.008 * math.pi / 2.0)
    return cosine * cosine


def update(time_ref, state_ref, pred_ref, new_state_ref, new_pred_ref):
    moment = jnp.broadcast_to(time_ref[0].astype(F32), (1, LANES))
    now, nxt = level(moment), level(moment - STRIDE)
    c1, c2 = jnp.sqrt(now), jnp.sqrt(nxt)
    c3 = jnp.sqrt(1.0 - nxt) / jnp.sqrt(1.0 - now)
    for j in range(pred_ref.shape[-1] // LANES):
        sl = slice(j * LANES, (j + 1) * LANES)
        p = pred_ref[0, :, sl]
        wide = p.astype(F32)
        st = state_ref[0, :, sl].astype(F32)
        new_pred_ref[0, :, sl] = p
        new_state_ref[0, :, sl] = (c2 * wide + c3 * (st - c1 * wide)).astype(BF16)


def per_device(
    sizes, state, prev_pred, ancestors, timestep, w_in, w_time, w_qkv, w_attn_out, w_up, w_down, w_out
):
    ndom, nrow = sizes
    _, rows, width = state.shape
    d, ch = w_out.shape
    cols, height, head = width // ch, rows * nrow, d // HEADS
    ff = w_up.shape[2]
    half = d // 2
    rates = np.exp(-math.log(10000.0) * np.arange(half) / half).astype(np.float32)
    cos_r, sin_r = rope_tables(cols, head)
    cos_c, sin_c = rope_tables(height, head)
    tables = jnp.asarray(
        np.concatenate(
            [
                cos_r, sin_r, np.repeat(cos_c, 8, axis=0), np.repeat(sin_c, 8, axis=0),
                np.tile(rates[None], (8, 1)),
            ]
        )
    )
    mine = cols // nrow
    wide = min(16, mine)
    flat = -(-wide * ch // LANES) * LANES
    halves, steps = mine // wide, max(rows // 2, 1)
    cfg = (ndom, nrow, rows, cols, ch, d, head, height, wide, flat)
    smem = pl.BlockSpec(memory_space=pltpu.SMEM)
    vmem = pl.BlockSpec(memory_space=pltpu.VMEM)
    hbm = pl.BlockSpec(memory_space=pl.ANY)
    whole = jax.ShapeDtypeStruct((1, rows, width), BF16)
    dma = pltpu.SemaphoreType.DMA
    chosen, predicted = pl.pallas_call(
        functools.partial(kernel, cfg),
        out_shape=(whole, whole),
        in_specs=[smem, smem, vmem, vmem, vmem, vmem, vmem, hbm, hbm, hbm, hbm, vmem],
        out_specs=(vmem, vmem),
        scratch_shapes=[
            pltpu.VMEM((2, d, 3 * d), BF16),
            pltpu.VMEM((2, d, d), BF16),
            pltpu.VMEM((2, d, ff), BF16),
            pltpu.VMEM((2, ff, d), BF16),
            pltpu.VMEM((rows * cols, LANES), F32),
            pltpu.VMEM((rows * cols, LANES), F32),
            pltpu.VMEM((rows, cols, d), BF16),
            pltpu.VMEM((height, mine, d), BF16),
            pltpu.VMEM((height * wide, LANES), F32),
            [pltpu.VMEM((ndom, height, flat), BF16)] * halves,
            pltpu.VMEM((height, flat), F32),
            pltpu.VMEM((halves, nrow, rows, flat), BF16),
            pltpu.VMEM((nrow, halves, rows, flat), BF16),
            pltpu.VMEM((ndom, rows, width), BF16),
            dma((2, 4)),
            dma,
            dma((ndom,)),
            dma((ndom,)),
            dma((steps, nrow)),
            dma((steps, nrow)),
            dma((halves, ndom)),
            dma((halves, ndom)),
            dma((halves, nrow)),
            dma((halves, nrow)),
        ],
        compiler_params=pltpu.CompilerParams(
            collective_id=0, has_side_effects=True, vmem_limit_bytes=56 * 1024 * 1024
        ),
    )(
        ancestors, timestep, state, prev_pred, tables, w_in, w_time,
        w_qkv, w_attn_out, w_up, w_down, w_out.T,
    )
    return pl.pallas_call(
        update,
        out_shape=(whole, whole),
        in_specs=[smem, vmem, vmem],
        out_specs=(vmem, vmem),
        compiler_params=pltpu.CompilerParams(vmem_limit_bytes=4 * 1024 * 1024),
    )(timestep, chosen, predicted)


def solution(mesh):
    part = P(("group", "dom"), "row", None)
    in_specs = (part, part, P("group"), P("group")) + (P(),) * 7
    return jax.shard_map(
        functools.partial(per_device, (mesh.shape["dom"], mesh.shape["row"])),
        mesh=mesh, in_specs=in_specs, out_specs=(part, part), check_vma=False,
    )
```

```python
import functools
import math

import jax
import jax.numpy as jnp
import numpy as np
from jax import lax
from jax.experimental import pallas as pl
from jax.experimental.pallas import tpu as pltpu
from jax.sharding import PartitionSpec as P

HEADS = 8
STEPS = 1000
STRIDE = 20
LANES = 128
MESH = pl.DeviceIdType.MESH
F32 = jnp.float32
BF16 = jnp.bfloat16


def rms(v):
    return v * lax.rsqrt(jnp.mean(v * v, axis=-1, keepdims=True) + 1e-06)


def mm(a, b):
    return jnp.dot(a, b, preferred_element_type=F32)


def mm_nt(a, b):
    return lax.dot_general(a, b, (((1,), (1,)), ((), ())), preferred_element_type=F32)


def rope_tables(length, head):
    half = head // 2
    rates = np.exp(-math.log(10000.0) * np.arange(half) / half)
    angles = np.arange(length)[:, None] * rates[None, :]
    reps = LANES // head
    cos = np.tile(np.concatenate([np.cos(angles), np.cos(angles)], axis=1), (1, reps))
    sin = np.tile(np.concatenate([-np.sin(angles), np.sin(angles)], axis=1), (1, reps))
    return cos.astype(np.float32), sin.astype(np.float32)


def rotated(v, cos, sin, head):
    inv = lax.rsqrt(jnp.mean(v * v, axis=-1, keepdims=True) + 1e-06)
    lane = lax.broadcasted_iota(jnp.int32, (1, LANES), 1)
    low = (lane % head) < head // 2
    parts = []
    for part in range(v.shape[1] // LANES):
        x = v[:, part * LANES : (part + 1) * LANES]
        partner = jnp.where(
            low,
            pltpu.roll(x, LANES - head // 2, 1),
            pltpu.roll(x, head // 2, 1),
        )
        parts.append((x * cos + partner * sin) * inv)
    return parts


def attention(q, k, v, mask, head):
    n = q[0].shape[0]
    lane = lax.broadcasted_iota(jnp.int32, (1, LANES), 1)
    per = LANES // head
    scale = math.log2(math.e) / math.sqrt(head)
    outs = []
    for part in range(len(q)):
        keys, vals = [], []
        for h in range(per):
            pick = jnp.where(lane // head == h, 1.0, 0.0).astype(BF16)
            keys.append(k[part] * pick)
            vals.append(
                jnp.concatenate([v[part] * pick, jnp.broadcast_to(pick, (n, LANES))], axis=1)
            )
        scores = mm_nt(q[part], jnp.concatenate(keys, axis=0))
        weights = jnp.exp2(scores * scale)
        if mask is not None:
            weights = weights * mask
        both = mm(weights.astype(BF16), jnp.concatenate(vals, axis=0))
        outs.append(both[:, :LANES] / both[:, LANES:])
    return jnp.concatenate(outs, axis=1).astype(BF16)


def mlp(h, w_up, w_down):
    lifted = mm(rms(h).astype(BF16), w_up)
    gated = jax.nn.gelu(lifted, approximate=True).astype(BF16)
    return (h + mm(gated, w_down)).astype(BF16)


def kernel(
    cfg,
    anc_ref, time_ref, state_ref, prev_ref, tab_ref, w_in_ref, w_time_ref,
    w_qkv_hbm, w_attn_hbm, w_up_hbm, w_down_hbm, w_out_ref,
    state_out, pred_out,
    w_qkv, w_attn, w_up, w_down,
    xs, xp, h1, hcol, ptok, gat, selw, sel, fin, states,
    w_sem, own_sem, st_send, st_recv, h_send, h_recv, g_send, g_recv, p_send, p_recv,
):
    ndom, nrow, rows, cols, ch, d, head, height, wide, flat = cfg
    dom, row = lax.axis_index("dom"), lax.axis_index("row")
    mine = cols // nrow
    group = LANES // math.gcd(ch, LANES)
    glanes = group * ch
    halves = mine // wide

    loads = []
    pairs = ((w_qkv_hbm, w_qkv), (w_attn_hbm, w_attn), (w_up_hbm, w_up), (w_down_hbm, w_down))
    for b in range(2):
        for i, (src, dst) in enumerate(pairs):
            copy = pltpu.make_async_copy(src.at[b], dst.at[b], w_sem.at[b, i])
            copy.start()
            loads.append(copy)

    barrier = pltpu.get_barrier_semaphore()
    for k in range(1, ndom):
        pl.semaphore_signal(
            barrier, inc=1, device_id={"dom": lax.rem(dom + k, ndom)}, device_id_type=MESH
        )
    for k in range(1, nrow):
        pl.semaphore_signal(
            barrier, inc=1, device_id={"row": lax.rem(row + k, nrow)}, device_id_type=MESH
        )
    own = pltpu.make_async_copy(state_ref.at[0], states.at[dom], own_sem)
    own.start()

    lane = lax.broadcasted_iota(jnp.int32, (rows, LANES), 1)

    def split(c, carry):
        base = pl.multiple_of(c * glanes, LANES)
        for ref, out in ((state_ref, xs), (prev_ref, xp)):
            tiles = [
                ref[0, :, pl.ds(pl.multiple_of(base + j * LANES, LANES), LANES)].astype(F32)
                for j in range(glanes // LANES)
            ]
            for t in range(group):
                j, off = divmod(t * ch, LANES)
                v = pltpu.roll(tiles[j], LANES - off, 1) if off else tiles[j]
                if off + ch > LANES:
                    v = jnp.where(lane < LANES - off, v, pltpu.roll(tiles[j + 1], LANES - off, 1))
                out[pl.ds(c * group + t, rows, stride=cols), :] = v
        return carry

    lax.fori_loop(0, cols // group, split, 0)

    moment = time_ref[0].astype(F32)
    half = d // 2
    angles = tab_ref[2 * cols + 16 * height :, :] * moment
    emb = jnp.concatenate([jnp.sin(angles), jnp.cos(angles)], axis=1)
    temb = jnp.dot(
        emb, w_time_ref[...].astype(F32),
        precision=lax.Precision.HIGHEST, preferred_element_type=F32,
    )[0:1]
    w_in = w_in_ref[...].astype(F32)
    w_in_s, w_in_p = w_in[:ch].astype(BF16), w_in[ch:].astype(BF16)

    pl.semaphore_wait(barrier, ndom - 1 + nrow - 1)
    sends = []
    for k in range(1, ndom):
        copy = pltpu.make_async_remote_copy(
            src_ref=state_ref.at[0],
            dst_ref=states.at[dom],
            send_sem=st_send.at[k],
            recv_sem=st_recv.at[k],
            device_id={"dom": lax.rem(dom + k, ndom)},
            device_id_type=MESH,
        )
        copy.start()
        sends.append(copy)

    for copy in loads[:4]:
        copy.wait()
    cos_r, sin_r = tab_ref[0:cols], tab_ref[cols : 2 * cols]
    step_rows = 2 if rows % 2 == 0 else 1
    n0 = step_rows * cols

    def h_copy(i, k):
        peer = lax.rem(row + k, nrow)
        return pltpu.make_async_remote_copy(
            src_ref=h1.at[pl.ds(i * step_rows, step_rows), pl.ds(pl.multiple_of(peer * mine, mine), mine), :],
            dst_ref=hcol.at[pl.ds(row * rows + i * step_rows, step_rows)],
            send_sem=h_send.at[i, k],
            recv_sem=h_recv.at[i, k],
            device_id={"row": peer},
            device_id_type=MESH,
        )

    def first(i, carry):
        sl = pl.ds(pl.multiple_of(i * n0, n0), n0)
        h = mm(xs[sl, :ch].astype(BF16), w_in_s) + mm(xp[sl, :ch].astype(BF16), w_in_p) + temb
        h = h.astype(BF16).astype(F32)
        qkv = mm(rms(h).astype(BF16), w_qkv[0])
        cos = jnp.concatenate([cos_r] * step_rows, axis=0)
        sin = jnp.concatenate([sin_r] * step_rows, axis=0)
        q = [x.astype(BF16) for x in rotated(qkv[:, :d], cos, sin, head)]
        k = [x.astype(BF16) for x in rotated(qkv[:, d : 2 * d], cos, sin, head)]
        v = qkv[:, 2 * d :].astype(BF16)
        v = [v[:, p * LANES : (p + 1) * LANES] for p in range(d // LANES)]
        mixed = []
        for r in range(step_rows):
            a, b = r * cols, (r + 1) * cols
            mixed.append(
                attention([x[a:b] for x in q], [x[a:b] for x in k], [x[a:b] for x in v], None, head)
            )
        o = jnp.concatenate(mixed, axis=0)
        h = (h + mm(o, w_attn[0])).astype(BF16).astype(F32)
        h = mlp(h, w_up[0], w_down[0])
        h1[pl.ds(i * step_rows, step_rows)] = h.reshape(step_rows, cols, d)
        for k in range(1, nrow):
            h_copy(i, k).start()
        return carry

    lax.fori_loop(0, rows // step_rows, first, 0)

    hcol[pl.ds(row * rows, rows)] = h1[:, pl.ds(pl.multiple_of(row * mine, mine), mine), :]
    for copy in loads[4:]:
        copy.wait()

    cos_c = tab_ref[2 * cols : 2 * cols + 8 * height].reshape(height, 8, LANES)
    sin_c = tab_ref[2 * cols + 8 * height : 2 * cols + 16 * height].reshape(height, 8, LANES)
    n1 = height * wide
    sub = height * 8
    cos_c = jnp.concatenate([cos_c] * (wide // 8), axis=1).reshape(n1, LANES)
    sin_c = jnp.concatenate([sin_c] * (wide // 8), axis=1).reshape(n1, LANES)
    per = LANES // head
    qi = lax.broadcasted_iota(jnp.int32, (sub, per * sub), 0)
    ki = lax.broadcasted_iota(jnp.int32, (sub, per * sub), 1)
    mask = jnp.where(qi % 8 == ki % 8, 1.0, 0.0).astype(F32)
    hlane = lax.broadcasted_iota(jnp.int32, (height, LANES), 1)

    for i in range(rows // step_rows):
        for k in range(1, nrow):
            h_copy(i, k).wait_recv()

    def g_copy(i, k):
        return pltpu.make_async_remote_copy(
            src_ref=gat[i].at[dom],
            dst_ref=gat[i].at[dom],
            send_sem=g_send.at[i, k],
            recv_sem=g_recv.at[i, k],
            device_id={"dom": lax.rem(dom + k, ndom)},
            device_id_type=MESH,
        )

    def second(i):
        sl = pl.ds(i * wide, wide)
        h = hcol[:, sl, :].reshape(n1, d).astype(F32)
        qkv = mm(rms(h).astype(BF16), w_qkv[1])
        q = rotated(qkv[:, :d], cos_c, sin_c, head)
        k = rotated(qkv[:, d : 2 * d], cos_c, sin_c, head)
        v = [qkv[:, 2 * d + p * LANES : 2 * d + (p + 1) * LANES] for p in range(d // LANES)]
        mixed = []
        for s in range(wide // 8):

            def cut(xs_):
                return [
                    x.reshape(height, wide, LANES)[:, 8 * s : 8 * s + 8, :]
                    .reshape(sub, LANES)
                    .astype(BF16)
                    for x in xs_
                ]

            o = attention(cut(q), cut(k), cut(v), mask, head)
            mixed.append(o.astype(F32).reshape(height, 8, d))
        o = jnp.concatenate(mixed, axis=1).reshape(n1, d).astype(BF16)
        h = (h + mm(o, w_attn[1])).astype(BF16).astype(F32)
        h = mlp(h, w_up[1], w_down[1]).astype(F32)
        ptok[:, 0:ch] = mm_nt(rms(h).astype(BF16), w_out_ref[...])
        toks = [ptok[pl.ds(t, height, stride=wide), :] for t in range(wide)]
        for j in range(flat // LANES):
            first_t = (j * LANES) // ch
            last_t = min((j * LANES + LANES - 1) // ch, wide - 1)
            acc = None
            for t in range(first_t, last_t + 1):
                s = t * ch - j * LANES
                x = pltpu.roll(toks[t], s % LANES, 1) if s % LANES else toks[t]
                acc = x if acc is None else jnp.where(hlane >= s, x, acc)
            gat[i][dom, :, j * LANES : (j + 1) * LANES] = acc.astype(BF16)
        for k in range(1, ndom):
            g_copy(i, k).start()

    for i in range(halves):
        second(i)

    own.wait()
    for copy in sends:
        copy.wait()
    a = anc_ref[dom]
    state_out[0] = states[a]

    def p_copy(i, k):
        peer = lax.rem(row + k, nrow)
        return pltpu.make_async_remote_copy(
            src_ref=sel.at[i, peer],
            dst_ref=fin.at[row, i],
            send_sem=p_send.at[i, k],
            recv_sem=p_recv.at[i, k],
            device_id={"row": peer},
            device_id_type=MESH,
        )

    for i in range(halves):
        for k in range(1, ndom):
            g_copy(i, k).wait_recv()
        selw[...] = gat[i][a].astype(F32)
        for r in range(nrow):
            sel[i, r] = selw[r * rows : (r + 1) * rows, :].astype(BF16)
        for k in range(1, nrow):
            p_copy(i, k).start()
        fin[row, i] = sel[i, row]
    for i in range(halves):
        for k in range(1, nrow):
            p_copy(i, k).wait_recv()

    size = wide * ch
    count = flat // LANES

    def piece(q, offset):
        r, i = divmod(q, halves)
        tile, rem = divmod(offset, LANES)

        def load(j):
            x = fin[r, i, :, j * LANES : (j + 1) * LANES].astype(F32)
            return pltpu.roll(x, LANES - rem, 1) if rem else x

        low = load(tile) if tile >= 0 else None
        if not rem or tile + 1 >= count:
            return low
        high = load(tile + 1)
        return high if low is None else jnp.where(lane < LANES - rem, low, high)

    for j in range(cols * ch // LANES):
        start = j * LANES
        acc = None
        for q in range(start // size, (start + LANES - 1) // size + 1):
            x = piece(q, start - q * size)
            acc = x if acc is None else jnp.where(lane >= q * size - start, x, acc)
        pred_out[0, :, start : start + LANES] = acc.astype(BF16)

    for i in range(rows // step_rows):
        for k in range(1, nrow):
            h_copy(i, k).wait_send()
    for i in range(halves):
        for k in range(1, ndom):
            g_copy(i, k).wait_send()
        for k in range(1, nrow):
            p_copy(i, k).wait_send()


def level(moment):
    cosine = jnp.cos((moment / STEPS + 0.008) / 1.008 * math.pi / 2.0)
    return cosine * cosine


def update(time_ref, state_ref, pred_ref, new_state_ref, new_pred_ref):
    moment = jnp.broadcast_to(time_ref[0].astype(F32), (1, LANES))
    now, nxt = level(moment), level(moment - STRIDE)
    c1, c2 = jnp.sqrt(now), jnp.sqrt(nxt)
    c3 = jnp.sqrt(1.0 - nxt) / jnp.sqrt(1.0 - now)
    for j in range(pred_ref.shape[-1] // LANES):
        sl = slice(j * LANES, (j + 1) * LANES)
        p = pred_ref[0, :, sl]
        wide = p.astype(F32)
        st = state_ref[0, :, sl].astype(F32)
        new_pred_ref[0, :, sl] = p
        new_state_ref[0, :, sl] = (c2 * wide + c3 * (st - c1 * wide)).astype(BF16)


def per_device(
    sizes, state, prev_pred, ancestors, timestep, w_in, w_time, w_qkv, w_attn_out, w_up, w_down, w_out
):
    ndom, nrow = sizes
    _, rows, width = state.shape
    d, ch = w_out.shape
    cols, height, head = width // ch, rows * nrow, d // HEADS
    ff = w_up.shape[2]
    half = d // 2
    rates = np.exp(-math.log(10000.0) * np.arange(half) / half).astype(np.float32)
    cos_r, sin_r = rope_tables(cols, head)
    cos_c, sin_c = rope_tables(height, head)
    tables = jnp.asarray(
        np.concatenate(
            [
                cos_r, sin_r, np.repeat(cos_c, 8, axis=0), np.repeat(sin_c, 8, axis=0),
                np.tile(rates[None], (8, 1)),
            ]
        )
    )
    mine = cols // nrow
    wide = min(16, mine)
    flat = -(-wide * ch // LANES) * LANES
    halves, steps = mine // wide, max(rows // 2, 1)
    cfg = (ndom, nrow, rows, cols, ch, d, head, height, wide, flat)
    smem = pl.BlockSpec(memory_space=pltpu.SMEM)
    vmem = pl.BlockSpec(memory_space=pltpu.VMEM)
    hbm = pl.BlockSpec(memory_space=pl.ANY)
    whole = jax.ShapeDtypeStruct((1, rows, width), BF16)
    dma = pltpu.SemaphoreType.DMA
    chosen, predicted = pl.pallas_call(
        functools.partial(kernel, cfg),
        out_shape=(pltpu.VMEM((1, rows, width), BF16),) * 2,
        in_specs=[smem, smem, vmem, vmem, vmem, vmem, vmem, hbm, hbm, hbm, hbm, vmem],
        out_specs=(vmem, vmem),
        scratch_shapes=[
            pltpu.VMEM((2, d, 3 * d), BF16),
            pltpu.VMEM((2, d, d), BF16),
            pltpu.VMEM((2, d, ff), BF16),
            pltpu.VMEM((2, ff, d), BF16),
            pltpu.VMEM((rows * cols, LANES), F32),
            pltpu.VMEM((rows * cols, LANES), F32),
            pltpu.VMEM((rows, cols, d), BF16),
            pltpu.VMEM((height, mine, d), BF16),
            pltpu.VMEM((height * wide, LANES), F32),
            [pltpu.VMEM((ndom, height, flat), BF16)] * halves,
            pltpu.VMEM((height, flat), F32),
            pltpu.VMEM((halves, nrow, rows, flat), BF16),
            pltpu.VMEM((nrow, halves, rows, flat), BF16),
            pltpu.VMEM((ndom, rows, width), BF16),
            dma((2, 4)),
            dma,
            dma((ndom,)),
            dma((ndom,)),
            dma((steps, nrow)),
            dma((steps, nrow)),
            dma((halves, ndom)),
            dma((halves, ndom)),
            dma((halves, nrow)),
            dma((halves, nrow)),
        ],
        compiler_params=pltpu.CompilerParams(
            collective_id=0, has_side_effects=True, vmem_limit_bytes=56 * 1024 * 1024
        ),
    )(
        ancestors, timestep, state, prev_pred, tables, w_in, w_time,
        w_qkv, w_attn_out, w_up, w_down, w_out.T,
    )
    return pl.pallas_call(
        update,
        out_shape=(whole, whole),
        in_specs=[smem, vmem, vmem],
        out_specs=(vmem, vmem),
        compiler_params=pltpu.CompilerParams(vmem_limit_bytes=4 * 1024 * 1024),
    )(timestep, chosen, predicted)


def solution(mesh):
    part = P(("group", "dom"), "row", None)
    in_specs = (part, part, P("group"), P("group")) + (P(),) * 7
    return jax.shard_map(
        functools.partial(per_device, (mesh.shape["dom"], mesh.shape["row"])),
        mesh=mesh, in_specs=in_specs, out_specs=(part, part), check_vma=False,
    )
```

```python
import functools
import math

import jax
import jax.numpy as jnp
import numpy as np
from jax import lax
from jax.experimental import pallas as pl
from jax.experimental.pallas import tpu as pltpu
from jax.sharding import PartitionSpec as P

HEADS = 8
STEPS = 1000
STRIDE = 20
LANES = 128
MESH = pl.DeviceIdType.MESH
F32 = jnp.float32
BF16 = jnp.bfloat16


def rms(v):
    return v * lax.rsqrt(jnp.mean(v * v, axis=-1, keepdims=True) + 1e-06)


def mm(a, b):
    return jnp.dot(a, b, preferred_element_type=F32)


def mm_nt(a, b):
    return lax.dot_general(a, b, (((1,), (1,)), ((), ())), preferred_element_type=F32)


def rope_tables(length, head):
    half = head // 2
    rates = np.exp(-math.log(10000.0) * np.arange(half) / half)
    angles = np.arange(length)[:, None] * rates[None, :]
    reps = LANES // head
    cos = np.tile(np.concatenate([np.cos(angles), np.cos(angles)], axis=1), (1, reps))
    sin = np.tile(np.concatenate([-np.sin(angles), np.sin(angles)], axis=1), (1, reps))
    return cos.astype(np.float32), sin.astype(np.float32)


def rotated(v, cos, sin, head):
    inv = lax.rsqrt(jnp.mean(v * v, axis=-1, keepdims=True) + 1e-06)
    lane = lax.broadcasted_iota(jnp.int32, (1, LANES), 1)
    low = (lane % head) < head // 2
    parts = []
    for part in range(v.shape[1] // LANES):
        x = v[:, part * LANES : (part + 1) * LANES]
        partner = jnp.where(
            low,
            pltpu.roll(x, LANES - head // 2, 1),
            pltpu.roll(x, head // 2, 1),
        )
        parts.append((x * cos + partner * sin) * inv)
    return parts


def attention(q, k, v, mask, head):
    n = q[0].shape[0]
    lane = lax.broadcasted_iota(jnp.int32, (1, LANES), 1)
    per = LANES // head
    scale = math.log2(math.e) / math.sqrt(head)
    outs = []
    for part in range(len(q)):
        keys, vals = [], []
        for h in range(per):
            pick = jnp.where(lane // head == h, 1.0, 0.0).astype(BF16)
            keys.append(k[part] * pick)
            vals.append(
                jnp.concatenate([v[part] * pick, jnp.broadcast_to(pick, (n, LANES))], axis=1)
            )
        scores = mm_nt(q[part], jnp.concatenate(keys, axis=0))
        weights = jnp.exp2(scores * scale)
        if mask is not None:
            weights = weights * mask
        both = mm(weights.astype(BF16), jnp.concatenate(vals, axis=0))
        outs.append(both[:, :LANES] / both[:, LANES:])
    return jnp.concatenate(outs, axis=1).astype(BF16)


def mlp(h, w_up, w_down):
    lifted = mm(rms(h).astype(BF16), w_up)
    gated = jax.nn.gelu(lifted, approximate=True).astype(BF16)
    return (h + mm(gated, w_down)).astype(BF16)


def kernel(
    cfg,
    anc_ref, time_ref, state_ref, prev_ref, tab_ref, w_in_ref, w_time_ref,
    w_qkv_hbm, w_attn_hbm, w_up_hbm, w_down_hbm, w_out_ref,
    state_out, pred_out,
    w_qkv, w_attn, w_up, w_down,
    xs, xp, h1, hcol, ptok, gat, selw, sel, fin, states,
    w_sem, own_sem, st_send, st_recv, h_send, h_recv, g_send, g_recv, p_send, p_recv,
):
    ndom, nrow, rows, cols, ch, d, head, height, wide, flat, pair = cfg
    dom, row = lax.axis_index("dom"), lax.axis_index("row")
    mine = cols // nrow
    group = LANES // math.gcd(ch, LANES)
    glanes = group * ch
    halves = mine // wide
    teams = ndom // pair
    team, seat = lax.div(dom, pair), lax.rem(dom, pair)

    loads = []
    pairs = ((w_qkv_hbm, w_qkv), (w_attn_hbm, w_attn), (w_up_hbm, w_up), (w_down_hbm, w_down))
    for b in range(2):
        for i, (src, dst) in enumerate(pairs):
            copy = pltpu.make_async_copy(src.at[b], dst.at[b], w_sem.at[b, i])
            copy.start()
            loads.append(copy)

    barrier = pltpu.get_barrier_semaphore()
    for k in range(1, ndom):
        pl.semaphore_signal(
            barrier, inc=1, device_id={"dom": lax.rem(dom + k, ndom)}, device_id_type=MESH
        )
    for e in range(teams):
        there = lax.rem(team + e, teams) * pair + seat
        for k in range(1, nrow):
            pl.semaphore_signal(
                barrier,
                inc=1,
                device_id={"dom": there, "row": lax.rem(row + k, nrow)},
                device_id_type=MESH,
            )
    own = pltpu.make_async_copy(state_ref.at[0], states.at[dom], own_sem)
    own.start()

    lane = lax.broadcasted_iota(jnp.int32, (rows, LANES), 1)

    def split(c, carry):
        base = pl.multiple_of(c * glanes, LANES)
        for ref, out in ((state_ref, xs), (prev_ref, xp)):
            tiles = [
                ref[0, :, pl.ds(pl.multiple_of(base + j * LANES, LANES), LANES)].astype(F32)
                for j in range(glanes // LANES)
            ]
            for t in range(group):
                j, off = divmod(t * ch, LANES)
                v = pltpu.roll(tiles[j], LANES - off, 1) if off else tiles[j]
                if off + ch > LANES:
                    v = jnp.where(lane < LANES - off, v, pltpu.roll(tiles[j + 1], LANES - off, 1))
                out[pl.ds(c * group + t, rows, stride=cols), :] = v
        return carry

    lax.fori_loop(0, cols // group, split, 0)

    moment = time_ref[0].astype(F32)
    half = d // 2
    angles = tab_ref[2 * cols + 16 * height :, :] * moment
    emb = jnp.concatenate([jnp.sin(angles), jnp.cos(angles)], axis=1)
    temb = jnp.dot(
        emb, w_time_ref[...].astype(F32),
        precision=lax.Precision.HIGHEST, preferred_element_type=F32,
    )[0:1]
    w_in = w_in_ref[...].astype(F32)
    w_in_s, w_in_p = w_in[:ch].astype(BF16), w_in[ch:].astype(BF16)

    pl.semaphore_wait(barrier, ndom - 1 + teams * (nrow - 1))
    sends = []
    for k in range(1, ndom):
        copy = pltpu.make_async_remote_copy(
            src_ref=state_ref.at[0],
            dst_ref=states.at[dom],
            send_sem=st_send.at[k],
            recv_sem=st_recv.at[k],
            device_id={"dom": lax.rem(dom + k, ndom)},
            device_id_type=MESH,
        )
        copy.start()
        sends.append(copy)

    for copy in loads[:4]:
        copy.wait()
    cos_r, sin_r = tab_ref[0:cols], tab_ref[cols : 2 * cols]
    step_rows = 2 if rows % 2 == 0 else 1
    n0 = step_rows * cols

    def h_copy(i, k):
        peer = lax.rem(row + k, nrow)
        return pltpu.make_async_remote_copy(
            src_ref=h1.at[pl.ds(i * step_rows, step_rows), pl.ds(pl.multiple_of(peer * mine, mine), mine), :],
            dst_ref=hcol.at[pl.ds(row * rows + i * step_rows, step_rows)],
            send_sem=h_send.at[i, k],
            recv_sem=h_recv.at[i, k],
            device_id={"row": peer},
            device_id_type=MESH,
        )

    def first(i, carry):
        sl = pl.ds(pl.multiple_of(i * n0, n0), n0)
        h = mm(xs[sl, :ch].astype(BF16), w_in_s) + mm(xp[sl, :ch].astype(BF16), w_in_p) + temb
        h = h.astype(BF16).astype(F32)
        qkv = mm(rms(h).astype(BF16), w_qkv[0])
        cos = jnp.concatenate([cos_r] * step_rows, axis=0)
        sin = jnp.concatenate([sin_r] * step_rows, axis=0)
        q = [x.astype(BF16) for x in rotated(qkv[:, :d], cos, sin, head)]
        k = [x.astype(BF16) for x in rotated(qkv[:, d : 2 * d], cos, sin, head)]
        v = qkv[:, 2 * d :].astype(BF16)
        v = [v[:, p * LANES : (p + 1) * LANES] for p in range(d // LANES)]
        mixed = []
        for r in range(step_rows):
            a, b = r * cols, (r + 1) * cols
            mixed.append(
                attention([x[a:b] for x in q], [x[a:b] for x in k], [x[a:b] for x in v], None, head)
            )
        o = jnp.concatenate(mixed, axis=0)
        h = (h + mm(o, w_attn[0])).astype(BF16).astype(F32)
        h = mlp(h, w_up[0], w_down[0])
        h1[pl.ds(i * step_rows, step_rows)] = h.reshape(step_rows, cols, d)
        for k in range(1, nrow):
            h_copy(i, k).start()
        return carry

    lax.fori_loop(0, rows // step_rows, first, 0)

    hcol[pl.ds(row * rows, rows)] = h1[:, pl.ds(pl.multiple_of(row * mine, mine), mine), :]
    for copy in loads[4:]:
        copy.wait()

    cos_c = tab_ref[2 * cols : 2 * cols + 8 * height].reshape(height, 8, LANES)
    sin_c = tab_ref[2 * cols + 8 * height : 2 * cols + 16 * height].reshape(height, 8, LANES)
    n1 = height * wide
    sub = height * 8
    cos_c = jnp.concatenate([cos_c] * (wide // 8), axis=1).reshape(n1, LANES)
    sin_c = jnp.concatenate([sin_c] * (wide // 8), axis=1).reshape(n1, LANES)
    per = LANES // head
    qi = lax.broadcasted_iota(jnp.int32, (sub, per * sub), 0)
    ki = lax.broadcasted_iota(jnp.int32, (sub, per * sub), 1)
    mask = jnp.where(qi % 8 == ki % 8, 1.0, 0.0).astype(F32)
    hlane = lax.broadcasted_iota(jnp.int32, (height, LANES), 1)

    for i in range(rows // step_rows):
        for k in range(1, nrow):
            h_copy(i, k).wait_recv()

    def g_copy(i, k):
        return pltpu.make_async_remote_copy(
            src_ref=gat[i].at[seat],
            dst_ref=gat[i].at[seat],
            send_sem=g_send.at[i, k],
            recv_sem=g_recv.at[i, k],
            device_id={"dom": team * pair + lax.rem(seat + k, pair)},
            device_id_type=MESH,
        )

    def second(i):
        sl = pl.ds(i * wide, wide)
        h = hcol[:, sl, :].reshape(n1, d).astype(F32)
        qkv = mm(rms(h).astype(BF16), w_qkv[1])
        q = rotated(qkv[:, :d], cos_c, sin_c, head)
        k = rotated(qkv[:, d : 2 * d], cos_c, sin_c, head)
        v = [qkv[:, 2 * d + p * LANES : 2 * d + (p + 1) * LANES] for p in range(d // LANES)]
        mixed = []
        for s in range(wide // 8):

            def cut(xs_):
                return [
                    x.reshape(height, wide, LANES)[:, 8 * s : 8 * s + 8, :]
                    .reshape(sub, LANES)
                    .astype(BF16)
                    for x in xs_
                ]

            o = attention(cut(q), cut(k), cut(v), mask, head)
            mixed.append(o.astype(F32).reshape(height, 8, d))
        o = jnp.concatenate(mixed, axis=1).reshape(n1, d).astype(BF16)
        h = (h + mm(o, w_attn[1])).astype(BF16).astype(F32)
        h = mlp(h, w_up[1], w_down[1]).astype(F32)
        ptok[:, 0:ch] = mm_nt(rms(h).astype(BF16), w_out_ref[...])
        toks = [ptok[pl.ds(t, height, stride=wide), :] for t in range(wide)]
        for j in range(flat // LANES):
            first_t = (j * LANES) // ch
            last_t = min((j * LANES + LANES - 1) // ch, wide - 1)
            acc = None
            for t in range(first_t, last_t + 1):
                s = t * ch - j * LANES
                x = pltpu.roll(toks[t], s % LANES, 1) if s % LANES else toks[t]
                acc = x if acc is None else jnp.where(hlane >= s, x, acc)
            gat[i][seat, :, j * LANES : (j + 1) * LANES] = acc.astype(BF16)
        for k in range(1, pair):
            g_copy(i, k).start()

    for i in range(halves):
        second(i)

    def p_copy(i, e, k):
        there, peer = lax.rem(team + e, teams), lax.rem(row + k, nrow)
        return pltpu.make_async_remote_copy(
            src_ref=sel.at[i, there, peer],
            dst_ref=fin[i].at[team, row],
            send_sem=p_send.at[i, e, k],
            recv_sem=p_recv.at[i, e, k],
            device_id={"dom": there * pair + seat, "row": peer},
            device_id_type=MESH,
        )

    others = [(e, k) for e in range(teams) for k in range(nrow) if (e, k) != (0, 0)]
    others.sort(key=lambda x: (x[0] == 0, x))
    for i in range(halves):
        for k in range(1, pair):
            g_copy(i, k).wait_recv()
        for e in [*range(1, teams), 0]:
            there = lax.rem(team + e, teams)
            want = anc_ref[there * pair + seat] - team * pair
            selw[...] = gat[i][jnp.clip(want, 0, pair - 1)].astype(F32)
            for r in range(nrow):
                sel[i, there, r] = selw[r * rows : (r + 1) * rows, :].astype(BF16)
            for k in range(nrow):
                if (e, k) != (0, 0):
                    p_copy(i, e, k).start()
        fin[i][team, row] = sel[i, team, row]

    own.wait()
    for copy in sends:
        copy.wait()
    a = anc_ref[dom]
    state_out[0] = states[a]
    home = lax.div(a, pair)

    for i in range(halves):
        for e, k in others:
            p_copy(i, e, k).wait_recv()

    size = wide * ch
    count = flat // LANES

    def piece(q, offset):
        r, i = divmod(q, halves)
        tile, rem = divmod(offset, LANES)

        def load(j):
            x = fin[i][home, r, :, j * LANES : (j + 1) * LANES].astype(F32)
            return pltpu.roll(x, LANES - rem, 1) if rem else x

        low = load(tile) if tile >= 0 else None
        if not rem or tile + 1 >= count:
            return low
        high = load(tile + 1)
        return high if low is None else jnp.where(lane < LANES - rem, low, high)

    for j in range(cols * ch // LANES):
        start = j * LANES
        acc = None
        for q in range(start // size, (start + LANES - 1) // size + 1):
            x = piece(q, start - q * size)
            acc = x if acc is None else jnp.where(lane >= q * size - start, x, acc)
        pred_out[0, :, start : start + LANES] = acc.astype(BF16)

    for i in range(rows // step_rows):
        for k in range(1, nrow):
            h_copy(i, k).wait_send()
    for i in range(halves):
        for k in range(1, pair):
            g_copy(i, k).wait_send()
        for e, k in others:
            p_copy(i, e, k).wait_send()


def level(moment):
    cosine = jnp.cos((moment / STEPS + 0.008) / 1.008 * math.pi / 2.0)
    return cosine * cosine


def update(time_ref, state_ref, pred_ref, new_state_ref, new_pred_ref):
    moment = jnp.broadcast_to(time_ref[0].astype(F32), (1, LANES))
    now, nxt = level(moment), level(moment - STRIDE)
    c1, c2 = jnp.sqrt(now), jnp.sqrt(nxt)
    c3 = jnp.sqrt(1.0 - nxt) / jnp.sqrt(1.0 - now)
    for j in range(pred_ref.shape[-1] // LANES):
        sl = slice(j * LANES, (j + 1) * LANES)
        p = pred_ref[0, :, sl]
        wide = p.astype(F32)
        st = state_ref[0, :, sl].astype(F32)
        new_pred_ref[0, :, sl] = p
        new_state_ref[0, :, sl] = (c2 * wide + c3 * (st - c1 * wide)).astype(BF16)


def per_device(
    sizes, state, prev_pred, ancestors, timestep, w_in, w_time, w_qkv, w_attn_out, w_up, w_down, w_out
):
    ndom, nrow = sizes
    _, rows, width = state.shape
    d, ch = w_out.shape
    cols, height, head = width // ch, rows * nrow, d // HEADS
    ff = w_up.shape[2]
    half = d // 2
    rates = np.exp(-math.log(10000.0) * np.arange(half) / half).astype(np.float32)
    cos_r, sin_r = rope_tables(cols, head)
    cos_c, sin_c = rope_tables(height, head)
    tables = jnp.asarray(
        np.concatenate(
            [
                cos_r, sin_r, np.repeat(cos_c, 8, axis=0), np.repeat(sin_c, 8, axis=0),
                np.tile(rates[None], (8, 1)),
            ]
        )
    )
    mine = cols // nrow
    wide = min(16, mine)
    flat = -(-wide * ch // LANES) * LANES
    halves, steps = mine // wide, max(rows // 2, 1)
    pair = max(p for p in range(1, ndom + 1) if ndom % p == 0 and p * p <= ndom)
    teams = ndom // pair
    cfg = (ndom, nrow, rows, cols, ch, d, head, height, wide, flat, pair)
    smem = pl.BlockSpec(memory_space=pltpu.SMEM)
    vmem = pl.BlockSpec(memory_space=pltpu.VMEM)
    hbm = pl.BlockSpec(memory_space=pl.ANY)
    whole = jax.ShapeDtypeStruct((1, rows, width), BF16)
    dma = pltpu.SemaphoreType.DMA
    chosen, predicted = pl.pallas_call(
        functools.partial(kernel, cfg),
        out_shape=(pltpu.VMEM((1, rows, width), BF16),) * 2,
        in_specs=[smem, smem, vmem, vmem, vmem, vmem, vmem, hbm, hbm, hbm, hbm, vmem],
        out_specs=(vmem, vmem),
        scratch_shapes=[
            pltpu.VMEM((2, d, 3 * d), BF16),
            pltpu.VMEM((2, d, d), BF16),
            pltpu.VMEM((2, d, ff), BF16),
            pltpu.VMEM((2, ff, d), BF16),
            pltpu.VMEM((rows * cols, LANES), F32),
            pltpu.VMEM((rows * cols, LANES), F32),
            pltpu.VMEM((rows, cols, d), BF16),
            pltpu.VMEM((height, mine, d), BF16),
            pltpu.VMEM((height * wide, LANES), F32),
            [pltpu.VMEM((pair, height, flat), BF16)] * halves,
            pltpu.VMEM((height, flat), F32),
            pltpu.VMEM((halves, teams, nrow, rows, flat), BF16),
            [pltpu.VMEM((teams, nrow, rows, flat), BF16)] * halves,
            pltpu.VMEM((ndom, rows, width), BF16),
            dma((2, 4)),
            dma,
            dma((ndom,)),
            dma((ndom,)),
            dma((steps, nrow)),
            dma((steps, nrow)),
            dma((halves, pair)),
            dma((halves, pair)),
            dma((halves, teams, nrow)),
            dma((halves, teams, nrow)),
        ],
        compiler_params=pltpu.CompilerParams(
            collective_id=0, has_side_effects=True, vmem_limit_bytes=56 * 1024 * 1024
        ),
    )(
        ancestors, timestep, state, prev_pred, tables, w_in, w_time,
        w_qkv, w_attn_out, w_up, w_down, w_out.T,
    )
    return pl.pallas_call(
        update,
        out_shape=(whole, whole),
        in_specs=[smem, vmem, vmem],
        out_specs=(vmem, vmem),
        compiler_params=pltpu.CompilerParams(vmem_limit_bytes=4 * 1024 * 1024),
    )(timestep, chosen, predicted)


def solution(mesh):
    part = P(("group", "dom"), "row", None)
    in_specs = (part, part, P("group"), P("group")) + (P(),) * 7
    return jax.shard_map(
        functools.partial(per_device, (mesh.shape["dom"], mesh.shape["row"])),
        mesh=mesh, in_specs=in_specs, out_specs=(part, part), check_vma=False,
    )
```

```python
import functools
import math

import jax
import jax.numpy as jnp
import numpy as np
from jax import lax
from jax.experimental import pallas as pl
from jax.experimental.pallas import tpu as pltpu
from jax.sharding import PartitionSpec as P

HEADS = 8
STEPS = 1000
STRIDE = 20
LANES = 128
MESH = pl.DeviceIdType.MESH
F32 = jnp.float32
BF16 = jnp.bfloat16


def rms(v):
    return v * lax.rsqrt(jnp.mean(v * v, axis=-1, keepdims=True) + 1e-06)


def mm(a, b):
    return jnp.dot(a, b, preferred_element_type=F32)


def mm_nt(a, b):
    return lax.dot_general(a, b, (((1,), (1,)), ((), ())), preferred_element_type=F32)


def rope_tables(length, head):
    half = head // 2
    rates = np.exp(-math.log(10000.0) * np.arange(half) / half)
    angles = np.arange(length)[:, None] * rates[None, :]
    reps = LANES // head
    cos = np.tile(np.concatenate([np.cos(angles), np.cos(angles)], axis=1), (1, reps))
    sin = np.tile(np.concatenate([-np.sin(angles), np.sin(angles)], axis=1), (1, reps))
    return cos.astype(np.float32), sin.astype(np.float32)


def rotated(v, cos, sin, head, scale=1.0):
    inv = lax.rsqrt(jnp.mean(v * v, axis=-1, keepdims=True) + 1e-06) * scale
    lane = lax.broadcasted_iota(jnp.int32, (1, LANES), 1)
    low = (lane % head) < head // 2
    parts = []
    for part in range(v.shape[1] // LANES):
        x = v[:, part * LANES : (part + 1) * LANES]
        partner = jnp.where(
            low,
            pltpu.roll(x, LANES - head // 2, 1),
            pltpu.roll(x, head // 2, 1),
        )
        parts.append((x * cos + partner * sin) * inv)
    return parts


def attention(q, k, v, mask, head):
    n = q[0].shape[0]
    lane = lax.broadcasted_iota(jnp.int32, (1, LANES), 1)
    per = LANES // head
    outs = []
    for part in range(len(q)):
        keys, vals = [], []
        for h in range(per):
            pick = jnp.where(lane // head == h, 1.0, 0.0).astype(BF16)
            keys.append(k[part] * pick)
            vals.append(
                jnp.concatenate([v[part] * pick, jnp.broadcast_to(pick, (n, LANES))], axis=1)
            )
        scores = mm_nt(q[part], jnp.concatenate(keys, axis=0))
        weights = jnp.exp2(scores)
        if mask is not None:
            weights = weights * mask
        both = mm(weights.astype(BF16), jnp.concatenate(vals, axis=0))
        outs.append(both[:, :LANES] / both[:, LANES:])
    return jnp.concatenate(outs, axis=1).astype(BF16)


def mlp(h, w_up, w_down):
    lifted = mm(rms(h).astype(BF16), w_up)
    root = math.sqrt(2.0 / math.pi)
    inner = lifted * (root + (root * 0.044715) * (lifted * lifted))
    half = 0.5 * lifted
    gated = (half + half * jnp.tanh(inner)).astype(BF16)
    return (h + mm(gated, w_down)).astype(BF16)


def kernel(
    cfg,
    anc_ref, time_ref, state_ref, prev_ref, tab_ref, w_in_ref, w_time_ref,
    w_qkv_hbm, w_attn_hbm, w_up_hbm, w_down_hbm, w_out_ref,
    state_out, pred_out,
    w_qkv, w_attn, w_up, w_down,
    xs, xp, h1, hcol, ptok, gat, selw, sel, fin, states,
    w_sem, own_sem, st_send, st_recv, h_send, h_recv, g_send, g_recv, p_send, p_recv,
):
    ndom, nrow, rows, cols, ch, d, head, height, wide, flat, pair = cfg
    dom, row = lax.axis_index("dom"), lax.axis_index("row")
    mine = cols // nrow
    group = LANES // math.gcd(ch, LANES)
    glanes = group * ch
    halves = mine // wide
    scale = math.log2(math.e) / math.sqrt(head)
    teams = ndom // pair
    team, seat = lax.div(dom, pair), lax.rem(dom, pair)

    loads = []
    pairs = ((w_qkv_hbm, w_qkv), (w_attn_hbm, w_attn), (w_up_hbm, w_up), (w_down_hbm, w_down))
    for b in range(2):
        for i, (src, dst) in enumerate(pairs):
            copy = pltpu.make_async_copy(src.at[b], dst.at[b], w_sem.at[b, i])
            copy.start()
            loads.append(copy)

    barrier = pltpu.get_barrier_semaphore()
    for k in range(1, ndom):
        pl.semaphore_signal(
            barrier, inc=1, device_id={"dom": lax.rem(dom + k, ndom)}, device_id_type=MESH
        )
    for e in range(teams):
        there = lax.rem(team + e, teams) * pair + seat
        for k in range(1, nrow):
            pl.semaphore_signal(
                barrier,
                inc=1,
                device_id={"dom": there, "row": lax.rem(row + k, nrow)},
                device_id_type=MESH,
            )
    own = pltpu.make_async_copy(state_ref.at[0], states.at[dom], own_sem)
    own.start()

    lane = lax.broadcasted_iota(jnp.int32, (rows, LANES), 1)

    def split(c, carry):
        base = pl.multiple_of(c * glanes, LANES)
        for ref, out in ((state_ref, xs), (prev_ref, xp)):
            tiles = [
                ref[0, :, pl.ds(pl.multiple_of(base + j * LANES, LANES), LANES)].astype(F32)
                for j in range(glanes // LANES)
            ]
            for t in range(group):
                j, off = divmod(t * ch, LANES)
                v = pltpu.roll(tiles[j], LANES - off, 1) if off else tiles[j]
                if off + ch > LANES:
                    v = jnp.where(lane < LANES - off, v, pltpu.roll(tiles[j + 1], LANES - off, 1))
                out[pl.ds(c * group + t, rows, stride=cols), :] = v
        return carry

    lax.fori_loop(0, cols // group, split, 0)

    moment = time_ref[0].astype(F32)
    half = d // 2
    times = jnp.broadcast_to(moment, (1, LANES))
    now, nxt = level(times), level(times - STRIDE)
    c1, c2 = jnp.sqrt(now), jnp.sqrt(nxt)
    c3 = jnp.sqrt(1.0 - nxt) / jnp.sqrt(1.0 - now)
    angles = tab_ref[2 * cols + 16 * height :, :] * moment
    emb = jnp.concatenate([jnp.sin(angles), jnp.cos(angles)], axis=1)
    temb = jnp.dot(
        emb, w_time_ref[...].astype(F32),
        precision=lax.Precision.HIGHEST, preferred_element_type=F32,
    )[0:1]
    w_in = w_in_ref[...].astype(F32)
    w_in_s, w_in_p = w_in[:ch].astype(BF16), w_in[ch:].astype(BF16)

    pl.semaphore_wait(barrier, ndom - 1 + teams * (nrow - 1))
    sends = []
    for k in range(1, ndom):
        copy = pltpu.make_async_remote_copy(
            src_ref=state_ref.at[0],
            dst_ref=states.at[dom],
            send_sem=st_send.at[k],
            recv_sem=st_recv.at[k],
            device_id={"dom": lax.rem(dom + k, ndom)},
            device_id_type=MESH,
        )
        copy.start()
        sends.append(copy)

    for copy in loads[:4]:
        copy.wait()
    cos_r, sin_r = tab_ref[0:cols], tab_ref[cols : 2 * cols]
    step_rows = 2 if rows % 2 == 0 else 1
    n0 = step_rows * cols

    def h_copy(i, k):
        peer = lax.rem(row + k, nrow)
        return pltpu.make_async_remote_copy(
            src_ref=h1.at[pl.ds(i * step_rows, step_rows), pl.ds(pl.multiple_of(peer * mine, mine), mine), :],
            dst_ref=hcol.at[pl.ds(row * rows + i * step_rows, step_rows)],
            send_sem=h_send.at[i, k],
            recv_sem=h_recv.at[i, k],
            device_id={"row": peer},
            device_id_type=MESH,
        )

    def first(i, carry):
        sl = pl.ds(pl.multiple_of(i * n0, n0), n0)
        h = mm(xs[sl, :ch].astype(BF16), w_in_s) + mm(xp[sl, :ch].astype(BF16), w_in_p) + temb
        h = h.astype(BF16).astype(F32)
        qkv = mm(rms(h).astype(BF16), w_qkv[0])
        cos = jnp.concatenate([cos_r] * step_rows, axis=0)
        sin = jnp.concatenate([sin_r] * step_rows, axis=0)
        q = [x.astype(BF16) for x in rotated(qkv[:, :d], cos, sin, head, scale)]
        k = [x.astype(BF16) for x in rotated(qkv[:, d : 2 * d], cos, sin, head)]
        v = qkv[:, 2 * d :].astype(BF16)
        v = [v[:, p * LANES : (p + 1) * LANES] for p in range(d // LANES)]
        mixed = []
        for r in range(step_rows):
            a, b = r * cols, (r + 1) * cols
            mixed.append(
                attention([x[a:b] for x in q], [x[a:b] for x in k], [x[a:b] for x in v], None, head)
            )
        o = jnp.concatenate(mixed, axis=0)
        h = (h + mm(o, w_attn[0])).astype(BF16).astype(F32)
        h = mlp(h, w_up[0], w_down[0])
        h1[pl.ds(i * step_rows, step_rows)] = h.reshape(step_rows, cols, d)
        for k in range(1, nrow):
            h_copy(i, k).start()
        return carry

    lax.fori_loop(0, rows // step_rows, first, 0)

    hcol[pl.ds(row * rows, rows)] = h1[:, pl.ds(pl.multiple_of(row * mine, mine), mine), :]
    for copy in loads[4:]:
        copy.wait()

    cos_c = tab_ref[2 * cols : 2 * cols + 8 * height].reshape(height, 8, LANES)
    sin_c = tab_ref[2 * cols + 8 * height : 2 * cols + 16 * height].reshape(height, 8, LANES)
    n1 = height * wide
    sub = height * 8
    cos_c = jnp.concatenate([cos_c] * (wide // 8), axis=1).reshape(n1, LANES)
    sin_c = jnp.concatenate([sin_c] * (wide // 8), axis=1).reshape(n1, LANES)
    per = LANES // head
    qi = lax.broadcasted_iota(jnp.int32, (sub, per * sub), 0)
    ki = lax.broadcasted_iota(jnp.int32, (sub, per * sub), 1)
    mask = jnp.where(qi % 8 == ki % 8, 1.0, 0.0).astype(F32)
    hlane = lax.broadcasted_iota(jnp.int32, (height, LANES), 1)

    for i in range(rows // step_rows):
        for k in range(1, nrow):
            h_copy(i, k).wait_recv()

    def g_copy(i, k):
        return pltpu.make_async_remote_copy(
            src_ref=gat[i].at[seat],
            dst_ref=gat[i].at[seat],
            send_sem=g_send.at[i, k],
            recv_sem=g_recv.at[i, k],
            device_id={"dom": team * pair + lax.rem(seat + k, pair)},
            device_id_type=MESH,
        )

    def second(i):
        sl = pl.ds(i * wide, wide)
        h = hcol[:, sl, :].reshape(n1, d).astype(F32)
        qkv = mm(rms(h).astype(BF16), w_qkv[1])
        q = rotated(qkv[:, :d], cos_c, sin_c, head, scale)
        k = rotated(qkv[:, d : 2 * d], cos_c, sin_c, head)
        v = [qkv[:, 2 * d + p * LANES : 2 * d + (p + 1) * LANES] for p in range(d // LANES)]
        mixed = []
        for s in range(wide // 8):

            def cut(xs_):
                return [
                    x.reshape(height, wide, LANES)[:, 8 * s : 8 * s + 8, :]
                    .reshape(sub, LANES)
                    .astype(BF16)
                    for x in xs_
                ]

            o = attention(cut(q), cut(k), cut(v), mask, head)
            mixed.append(o.astype(F32).reshape(height, 8, d))
        o = jnp.concatenate(mixed, axis=1).reshape(n1, d).astype(BF16)
        h = (h + mm(o, w_attn[1])).astype(BF16).astype(F32)
        h = mlp(h, w_up[1], w_down[1]).astype(F32)
        ptok[:, 0:ch] = mm_nt(rms(h).astype(BF16), w_out_ref[...])
        toks = [ptok[pl.ds(t, height, stride=wide), :] for t in range(wide)]
        for j in range(flat // LANES):
            first_t = (j * LANES) // ch
            last_t = min((j * LANES + LANES - 1) // ch, wide - 1)
            acc = None
            for t in range(first_t, last_t + 1):
                s = t * ch - j * LANES
                x = pltpu.roll(toks[t], s % LANES, 1) if s % LANES else toks[t]
                acc = x if acc is None else jnp.where(hlane >= s, x, acc)
            gat[i][seat, :, j * LANES : (j + 1) * LANES] = acc.astype(BF16)
        for k in range(1, pair):
            g_copy(i, k).start()

    for i in range(halves):
        second(i)

    def p_copy(i, e, k):
        there, peer = lax.rem(team + e, teams), lax.rem(row + k, nrow)
        return pltpu.make_async_remote_copy(
            src_ref=sel.at[i, there, peer],
            dst_ref=fin[i].at[team, row],
            send_sem=p_send.at[i, e, k],
            recv_sem=p_recv.at[i, e, k],
            device_id={"dom": there * pair + seat, "row": peer},
            device_id_type=MESH,
        )

    others = [(e, k) for e in range(teams) for k in range(nrow) if (e, k) != (0, 0)]
    others.sort(key=lambda x: (x[0] == 0, x))
    for i in range(halves):
        for k in range(1, pair):
            g_copy(i, k).wait_recv()
        for e in [*range(1, teams), 0]:
            there = lax.rem(team + e, teams)
            want = anc_ref[there * pair + seat] - team * pair
            selw[...] = gat[i][jnp.clip(want, 0, pair - 1)].astype(F32)
            for r in range(nrow):
                sel[i, there, r] = selw[r * rows : (r + 1) * rows, :].astype(BF16)
            for k in range(nrow):
                if (e, k) != (0, 0):
                    p_copy(i, e, k).start()
        fin[i][team, row] = sel[i, team, row]

    own.wait()
    for copy in sends:
        copy.wait()
    a = anc_ref[dom]
    home = lax.div(a, pair)

    for i in range(halves):
        for e, k in others:
            p_copy(i, e, k).wait_recv()

    size = wide * ch
    count = flat // LANES

    def piece(q, offset):
        r, i = divmod(q, halves)
        tile, rem = divmod(offset, LANES)

        def load(j):
            x = fin[i][home, r, :, j * LANES : (j + 1) * LANES].astype(F32)
            return pltpu.roll(x, LANES - rem, 1) if rem else x

        low = load(tile) if tile >= 0 else None
        if not rem or tile + 1 >= count:
            return low
        high = load(tile + 1)
        return high if low is None else jnp.where(lane < LANES - rem, low, high)

    for j in range(cols * ch // LANES):
        start = j * LANES
        acc = None
        for q in range(start // size, (start + LANES - 1) // size + 1):
            x = piece(q, start - q * size)
            acc = x if acc is None else jnp.where(lane >= q * size - start, x, acc)
        acc = acc.astype(BF16)
        pred_out[0, :, start : start + LANES] = acc
        pred = acc.astype(F32)
        old = states[a, :, start : start + LANES].astype(F32)
        state_out[0, :, start : start + LANES] = (c2 * pred + c3 * (old - c1 * pred)).astype(BF16)

    for i in range(rows // step_rows):
        for k in range(1, nrow):
            h_copy(i, k).wait_send()
    for i in range(halves):
        for k in range(1, pair):
            g_copy(i, k).wait_send()
        for e, k in others:
            p_copy(i, e, k).wait_send()


def level(moment):
    cosine = jnp.cos((moment / STEPS + 0.008) / 1.008 * math.pi / 2.0)
    return cosine * cosine


def hand_out(state_ref, pred_ref, new_state_ref, new_pred_ref, sems):
    first = pltpu.make_async_copy(state_ref, new_state_ref, sems.at[0])
    second = pltpu.make_async_copy(pred_ref, new_pred_ref, sems.at[1])
    first.start()
    second.start()
    first.wait()
    second.wait()


def per_device(
    sizes, state, prev_pred, ancestors, timestep, w_in, w_time, w_qkv, w_attn_out, w_up, w_down, w_out
):
    ndom, nrow = sizes
    _, rows, width = state.shape
    d, ch = w_out.shape
    cols, height, head = width // ch, rows * nrow, d // HEADS
    ff = w_up.shape[2]
    half = d // 2
    rates = np.exp(-math.log(10000.0) * np.arange(half) / half).astype(np.float32)
    cos_r, sin_r = rope_tables(cols, head)
    cos_c, sin_c = rope_tables(height, head)
    tables = jnp.asarray(
        np.concatenate(
            [
                cos_r, sin_r, np.repeat(cos_c, 8, axis=0), np.repeat(sin_c, 8, axis=0),
                np.tile(rates[None], (8, 1)),
            ]
        )
    )
    mine = cols // nrow
    wide = min(16, mine)
    flat = -(-wide * ch // LANES) * LANES
    halves, steps = mine // wide, max(rows // 2, 1)
    pair = max(p for p in range(1, ndom + 1) if ndom % p == 0 and p * p <= ndom)
    teams = ndom // pair
    cfg = (ndom, nrow, rows, cols, ch, d, head, height, wide, flat, pair)
    smem = pl.BlockSpec(memory_space=pltpu.SMEM)
    vmem = pl.BlockSpec(memory_space=pltpu.VMEM)
    hbm = pl.BlockSpec(memory_space=pl.ANY)
    whole = jax.ShapeDtypeStruct((1, rows, width), BF16)
    dma = pltpu.SemaphoreType.DMA
    stepped, predicted = pl.pallas_call(
        functools.partial(kernel, cfg),
        out_shape=(pltpu.VMEM((1, rows, width), BF16),) * 2,
        in_specs=[smem, smem, vmem, vmem, vmem, vmem, vmem, hbm, hbm, hbm, hbm, vmem],
        out_specs=(vmem, vmem),
        scratch_shapes=[
            pltpu.VMEM((2, d, 3 * d), BF16),
            pltpu.VMEM((2, d, d), BF16),
            pltpu.VMEM((2, d, ff), BF16),
            pltpu.VMEM((2, ff, d), BF16),
            pltpu.VMEM((rows * cols, LANES), F32),
            pltpu.VMEM((rows * cols, LANES), F32),
            pltpu.VMEM((rows, cols, d), BF16),
            pltpu.VMEM((height, mine, d), BF16),
            pltpu.VMEM((height * wide, LANES), F32),
            [pltpu.VMEM((pair, height, flat), BF16)] * halves,
            pltpu.VMEM((height, flat), F32),
            pltpu.VMEM((halves, teams, nrow, rows, flat), BF16),
            [pltpu.VMEM((teams, nrow, rows, flat), BF16)] * halves,
            pltpu.VMEM((ndom, rows, width), BF16),
            dma((2, 4)),
            dma,
            dma((ndom,)),
            dma((ndom,)),
            dma((steps, nrow)),
            dma((steps, nrow)),
            dma((halves, pair)),
            dma((halves, pair)),
            dma((halves, teams, nrow)),
            dma((halves, teams, nrow)),
        ],
        compiler_params=pltpu.CompilerParams(
            collective_id=0, has_side_effects=True, vmem_limit_bytes=56 * 1024 * 1024
        ),
    )(
        ancestors, timestep, state, prev_pred, tables, w_in, w_time,
        w_qkv, w_attn_out, w_up, w_down, w_out.T,
    )
    return pl.pallas_call(
        hand_out,
        out_shape=(whole, whole),
        in_specs=[vmem, vmem],
        out_specs=(hbm, hbm),
        scratch_shapes=[dma((2,))],
        compiler_params=pltpu.CompilerParams(vmem_limit_bytes=4 * 1024 * 1024),
    )(stepped, predicted)


def solution(mesh):
    part = P(("group", "dom"), "row", None)
    in_specs = (part, part, P("group"), P("group")) + (P(),) * 7
    return jax.shard_map(
        functools.partial(per_device, (mesh.shape["dom"], mesh.shape["row"])),
        mesh=mesh, in_specs=in_specs, out_specs=(part, part), check_vma=False,
    )
```
